128 devices in a mesh: comp: 4 (over x), dom: 32 (over y, z, core).
Axes of the slice: x: 4, y: 4, z: 4, core: 2. Of those that a mesh axis runs over, the one named last changes fastest.
Arguments:
- atm_state: float32 [4, 4, 128, 16, 4096], P('comp', None, None, None, 'dom'), may hold values from -6 to 6
- elem_nbr: int32 [4, 4, 4096], P('comp', None, 'dom'), may hold values from 0 to 12287, as said below
- elem_metric: float32 [4, 16, 4096], P('comp', None, 'dom'), may hold values from 0.02 to 0.2
- bulk_coef: float32 [4, 16, 4096], P('comp', None, 'dom'), may hold values from 0.2 to 2
- stiffness: float32 [16, 16], replicated, may hold values from -1.5 to 1.5
- coupling: float32 [4, 16, 16], replicated, may hold values from -1.5 to 1.5
- atm_vertical: float32 [128, 128], replicated, may hold values from -0.25 to 0.25
- ocean_state: float32 [4, 4, 80, 32768], P('comp', None, None, 'dom'), may hold values from -6 to 6
- cell_nbr: int32 [4, 6, 32768], P('comp', None, 'dom'), may hold values from 0 to 32767, as said below
- cell_diff: float32 [4, 6, 32768], P('comp', None, 'dom'), may hold values from 0.01 to 0.12
- ocean_vertical: float32 [80, 80], replicated, may hold values from -0.3125 to 0.3125
- sea_mask: int32 [4, 32768], P('comp', 'dom'), may hold values 0 or 1
- pair_owner: int32 [4, 1024, 1], P('comp', 'dom'), may hold values from 0 to 31, as said below
- pair_block: int32 [4, 1024], P('comp', 'dom'), may hold values from 0 to 7
- pair_src: int32 [4, 1024], P('comp', 'dom'), may hold values from 0 to 15
- remap_weight: float32 [4, 1024, 128, 128], P('comp', 'dom'), may hold values from -0.5 to 0.5
Outputs:
- atm_next: float32 [4, 4, 128, 16, 4096], P('comp', None, None, None, 'dom')
- ocean_next: float32 [4, 4, 80, 32768], P('comp', None, None, 'dom')
The draws below stay inside these ranges and needn't reach their ends.
Inputs may be any that keep to these rules, and one draw needn't show every extreme that they name: `elem_nbr`: each entry of the slabs c < 3 differs from its own element index c * 4096 + e by 1 to 8; the last slab repeats the first. `cell_nbr`: each entry differs from its own cell index by 1 to 128; all slabs are equal. `pair_owner`: within the rows of one device (aligned blocks of 32 rows) no owner is named by more than 2 rows; the owners one below and one above that device's index of dom (counted round) are each named by exactly 2 rows.
All inputs are finite; a program needn't handle non-finite values. No bound on the sum of `sea_mask` on one device may be relied on, other than what follows from the above.
Results may differ from the reference program's by a relative error of at most 0.0001.
Values sent between devices are 32-bit elements; how exact they have to be, the bound alone decides.
A program may use at most 128 MiB of HBM per device.

```python
import math
import jax
import jax.numpy as jnp
from jax import lax

FIELDS = 4
LEV = 128
NPTS = 16
E_DEV = 128
RIM = 8
BLK = 128
OLEV = 80
HALO_O = 128
NBR_O = 6
PAIRS_DEV = 32
CAP = 2
COMPS = 4
NE = 4096
ATM_ELEMS = 12288
NC = 32768
SRC_BLOCKS = 16
OC_BLOCKS = 8
N_DOM = 32


def neighbour_table(key, count, total, reach):
    first, second = jax.random.split(key)
    own = jnp.arange(total, dtype=jnp.int32)[None, :]
    offset = jax.random.randint(first, (count, total), 1, reach + 1).astype(jnp.int32)
    offset = offset * (jax.random.randint(second, (count, total), 0, 2).astype(jnp.int32) * 2 - 1)
    raw = own + offset
    outside = (raw < 0) | (raw >= total)
    return jnp.where(outside, own - offset, raw).astype(jnp.int32)


def draw_elem_nbr(key, part):
    table = neighbour_table(jax.random.fold_in(key, 11), 4, ATM_ELEMS, RIM)
    slabs = jnp.transpose(table.reshape(4, COMPS - 1, NE), (1, 0, 2))
    return jnp.concatenate([slabs, slabs[:1]], axis=0)


def draw_cell_nbr(key, part):
    table = neighbour_table(jax.random.fold_in(key, 23), NBR_O, NC, HALO_O)
    return jnp.broadcast_to(table[None], (COMPS, NBR_O, NC))


def draw_pair_owner(key, part):
    base = jax.random.fold_in(key, 31)
    spare = (N_DOM - 2) * CAP

    def one_group(group_id):
        group_key = jax.random.fold_in(base, group_id)
        first, second = jax.random.split(group_key)
        home = group_id % N_DOM
        below = jnp.full((CAP,), (home - 1 + N_DOM) % N_DOM, jnp.int32)
        above = jnp.full((CAP,), (home + 1) % N_DOM, jnp.int32)
        step_away = (2 + jnp.arange(spare, dtype=jnp.int32) // CAP) % (N_DOM - 1)
        others = ((home + step_away) % N_DOM).astype(jnp.int32)
        picked = jnp.take(others, jax.random.permutation(first, spare))[:PAIRS_DEV - 2 * CAP]
        rows = jnp.concatenate([below, above, picked]).astype(jnp.int32)
        return jnp.take(rows, jax.random.permutation(second, PAIRS_DEV)).astype(jnp.int32)
    table = jax.vmap(one_group)(jnp.arange(COMPS * N_DOM, dtype=jnp.int32))
    return table.reshape(COMPS, N_DOM * PAIRS_DEV, 1).astype(jnp.int32)


def with_ends(values, own_key, least, top_value):
    index_at = [jax.random.randint(jax.random.fold_in(own_key, axis), (), 0, length) for axis, length in enumerate(values.shape)]
    longest = values.shape.index(max(values.shape))
    neighbour = index_at[:longest] + [(index_at[longest] + 1) % values.shape[longest]] + index_at[longest + 1:]
    return values.at[tuple(index_at)].set(least).at[tuple(neighbour)].set(top_value)


def steps_of(own_key, dims, shards, smallest, high):
    factor_of, own = 1.0, jax.random.fold_in(own_key, 6)
    for position, shards_of in shards:
        draws = jnp.exp(jax.random.uniform(jax.random.fold_in(own, position), (shards_of,), jnp.float32, smallest / len(shards), high / len(shards)))
        factor_of = factor_of * jnp.repeat(draws, dims[position] // shards_of).reshape([-1 if axis == position else 1 for axis in range(len(dims))])
    return factor_of


def scatter_about(rng, dims, deviation, most, pieces=(), kind=jnp.bfloat16):
    drawn = deviation * jax.random.normal(rng, dims, jnp.float32)
    if pieces:
        drawn = drawn * steps_of(rng, dims, pieces, -0.22, 0.18)
    return jnp.clip(drawn, -most, most).astype(kind)


def setup_inputs(seed: int = 0) -> dict:
    streams_of = jax.random.split(jax.random.key(seed), 17)
    return {
        "atm_state": scatter_about(streams_of[0], (COMPS, FIELDS, LEV, NPTS, NE), 1.0, 6.0, ((0, 4), (4, 32)), jnp.float32),
        "elem_nbr": draw_elem_nbr(jax.random.fold_in(streams_of[16], 71), 0),
        "elem_metric": jnp.clip(jnp.exp(math.log(0.2) - 2.3025851 * jax.random.uniform(streams_of[2], (COMPS, NPTS, NE), jnp.float32) ** steps_of(streams_of[2], (COMPS, NPTS, NE), ((0, 4), (2, 32)), -0.2, 0.2)), 0.02, 0.2),
        "bulk_coef": jnp.clip(jnp.exp(math.log(2.0) - 2.3025851 * jax.random.uniform(streams_of[3], (COMPS, NPTS, NE), jnp.float32) ** steps_of(streams_of[3], (COMPS, NPTS, NE), ((0, 4), (2, 32)), -0.2, 0.2)), 0.2, 2.0),
        "stiffness": scatter_about(streams_of[4], (NPTS, NPTS), NPTS ** -0.5, 1.5, (), jnp.float32),
        "coupling": scatter_about(streams_of[5], (4, NPTS, NPTS), NPTS ** -0.5, 1.5, (), jnp.float32),
        "atm_vertical": scatter_about(streams_of[6], (LEV, LEV), (4 * LEV) ** -0.5, 0.25, (), jnp.float32),
        "ocean_state": scatter_about(streams_of[7], (COMPS, FIELDS, OLEV, NC), 1.0, 6.0, ((0, 4), (3, 32)), jnp.float32),
        "cell_nbr": draw_cell_nbr(jax.random.fold_in(streams_of[16], 71), 0),
        "cell_diff": jnp.clip(jnp.exp(math.log(0.12) - 2.4849066 * jax.random.uniform(streams_of[9], (COMPS, NBR_O, NC), jnp.float32) ** steps_of(streams_of[9], (COMPS, NBR_O, NC), ((0, 4), (2, 32)), -0.2, 0.2)), 0.01, 0.12),
        "ocean_vertical": scatter_about(streams_of[10], (OLEV, OLEV), (4 * OLEV) ** -0.5, 0.3125, (), jnp.float32),
        "sea_mask": with_ends((jax.random.randint(streams_of[11], (COMPS, NC), 0, 4) < 3).astype(jnp.int32), jax.random.fold_in(streams_of[11], 1), 0, 1),
        "pair_owner": draw_pair_owner(jax.random.fold_in(streams_of[16], 71), 0),
        "pair_block": with_ends(jax.random.randint(streams_of[13], (COMPS, N_DOM * PAIRS_DEV), 0, OC_BLOCKS), jax.random.fold_in(streams_of[13], 1), 0, OC_BLOCKS - 1).astype(jnp.int32),
        "pair_src": with_ends(jax.random.randint(streams_of[14], (COMPS, N_DOM * PAIRS_DEV), 0, SRC_BLOCKS), jax.random.fold_in(streams_of[14], 1), 0, SRC_BLOCKS - 1).astype(jnp.int32),
        "remap_weight": scatter_about(streams_of[15], (COMPS, N_DOM * PAIRS_DEV, BLK, BLK), BLK ** -0.5, 0.5, ((0, 4), (1, 32)), jnp.float32),
    }


highest = lax.Precision.HIGHEST


def reference(atm_state, elem_nbr, elem_metric, bulk_coef, stiffness, coupling, atm_vertical, ocean_state, cell_nbr, cell_diff, ocean_vertical, sea_mask, pair_owner, pair_block, pair_src, remap_weight):
    live = COMPS - 1
    fields = atm_state.shape[1]
    levels = atm_state.shape[2]
    points = atm_state.shape[3]
    state = jnp.transpose(atm_state[:live], (1, 2, 3, 0, 4)).reshape(fields, levels, points, ATM_ELEMS)
    metric = jnp.transpose(elem_metric[:live], (1, 0, 2)).reshape(points, ATM_ELEMS)
    coef = jnp.transpose(bulk_coef[:live], (1, 0, 2)).reshape(points, ATM_ELEMS)
    neighbours = jnp.transpose(elem_nbr[:live], (1, 0, 2)).reshape(4, ATM_ELEMS)
    ocean = ocean_state[COMPS - 1]
    cell_table = cell_nbr[COMPS - 1]
    diffusion = cell_diff[COMPS - 1]
    sea = sea_mask[COMPS - 1]
    owner = pair_owner[:live, :, 0].reshape(-1)
    target = (owner * OC_BLOCKS + pair_block[:live].reshape(-1)).astype(jnp.int32)
    source = pair_src[:live].reshape(-1)
    weights = remap_weight[:live].reshape(-1, BLK, BLK)
    group = (jnp.arange(owner.shape[0], dtype=jnp.int32) // PAIRS_DEV).astype(jnp.int32)
    per_row = E_DEV // BLK
    point_of = (source // per_row).astype(jnp.int32)
    block_of = (group * per_row + source % per_row).astype(jnp.int32)
    atm_blocks = ATM_ELEMS // BLK
    top = ocean[:, 0, :].reshape(fields, NC // BLK, BLK)
    picked = top[:, target, :]
    contrib = jnp.einsum("fpo,pao->fpa", picked, weights, precision=highest)
    surface = jnp.zeros((fields, points, atm_blocks, BLK), jnp.float32)
    surface = surface.at[:, point_of, block_of].add(contrib).reshape(fields, points, ATM_ELEMS)
    flux = coef[None] * (state[:, levels - 1] - surface)
    flux_blocks = flux.reshape(fields, points, atm_blocks, BLK)[:, point_of, block_of]
    sent = jnp.einsum("fpa,pao->fpo", flux_blocks, weights, precision=highest)
    oflux = jnp.zeros((fields, NC // BLK, BLK), jnp.float32).at[:, target].add(sent).reshape(fields, NC)
    for step in range(2):
        tend = jnp.einsum("pq,flqe->flpe", stiffness, state, precision=highest)
        tend = tend + jnp.einsum("lm,fmpe->flpe", atm_vertical, state, precision=highest)
        for side in range(4):
            beside = jnp.take(state, neighbours[side], axis=3)
            tend = tend + jnp.einsum("pq,flqe->flpe", coupling[side], beside, precision=highest)
        state = state + metric[None, None] * tend
        state = state.at[:, levels - 1].add(-0.5 * flux)
    lap = jnp.zeros_like(ocean)
    for side in range(cell_table.shape[0]):
        lap = lap + diffusion[side][None, None] * (jnp.take(ocean, cell_table[side], axis=2) - ocean)
    fresh = ocean + lap + jnp.einsum("lm,fmc->flc", ocean_vertical, ocean, precision=highest)
    fresh = fresh.at[:, 0].add(0.5 * oflux)
    fresh = jnp.where(sea[None, None] == 1, fresh, ocean)
    atm_part = jnp.transpose(state.reshape(fields, levels, points, live, NE), (3, 0, 1, 2, 4))
    atm_next = jnp.concatenate([atm_part, jnp.zeros((1, fields, levels, points, NE), jnp.float32)], axis=0)
    ocean_next = jnp.concatenate([jnp.zeros((live,) + ocean.shape, jnp.float32), fresh[None]], axis=0)
    return (atm_next, ocean_next)
```

```python
import functools

import jax
import jax.numpy as jnp
from jax import lax
from jax.experimental import pallas as pl
from jax.experimental.pallas import tpu as pltpu
from jax.sharding import PartitionSpec as P

f32, bf16, i32 = jnp.float32, jnp.bfloat16, jnp.int32
FIELDS, LEV, NPTS, ELEMS = 4, 128, 16, 128
ROWS = FIELDS * LEV
BLOCKS, WIDTH = 8, 16
LANES = NPTS * WIDTH
SLABS, DOM = 4, 32
ATM = SLABS - 1
PAIRS, BLK = 32, 128
OLEV, CELLS, NBR_O = 80, 1024, 6
OROWS = FIELDS * OLEV
OBLOCKS = CELLS // BLK
MESH = pl.DeviceIdType.MESH
highest = lax.Precision.HIGHEST


def iota(shape, axis):
    return lax.broadcasted_iota(i32, shape, axis)


def swap_chunks(a):
    chunk = iota(a[0].shape, 1) // WIDTH
    a = [a[q] if q == 0 else pltpu.roll(a[q], WIDTH * q, 1) for q in range(8)]
    for k in (1, 2, 4):
        take = (chunk & k) != 0
        a = [jnp.where(take, a[(i + k) % 8], a[i]) for i in range(8)]
    out = [a[(-b) % 8] for b in range(8)]
    return [out[b] if b == 0 else pltpu.roll(out[b], 128 - WIDTH * b, 1) for b in range(8)]


def split(x):
    hi = x.astype(bf16)
    return hi, (x - hi.astype(f32)).astype(bf16)


def pick_rows(onehot, x):
    hi, lo = split(x)
    return jnp.dot(onehot, hi, preferred_element_type=f32) + jnp.dot(
        onehot, lo, preferred_element_type=f32
    )


def pack(f, st, x, xh, xl):
    def body(i, _):
        row = f * LEV + i * 16
        for h in range(2):
            a = [st[pl.ds(row * NPTS + h * 8 + q, 16, stride=NPTS), :] for q in range(8)]
            w = swap_chunks(a)
            cols = slice(h * 128, (h + 1) * 128)
            for b in range(BLOCKS):
                hi, lo = split(w[b])
                x[b, pl.ds(row, 16), cols] = w[b]
                xh[b + 1, pl.ds(row, 16), cols] = hi
                xl[b + 1, pl.ds(row, 16), cols] = lo
        return 0

    lax.fori_loop(0, LEV // 16, body, 0, unroll=2)


def unpack(f, x, st):
    def body(i, _):
        row = f * LEV + i * 16
        for h in range(2):
            cols = slice(h * 128, (h + 1) * 128)
            w = swap_chunks([x[b, pl.ds(row, 16), cols] for b in range(BLOCKS)])
            for q in range(8):
                st[pl.ds(row * NPTS + h * 8 + q, 16, stride=NPTS), :] = w[q]
        return 0

    lax.fori_loop(0, LEV // 16, body, 0, unroll=2)


def small_tables(first, nbr, metric, stiff, coup, vert, cr, met, near, vv):
    spread = (iota((NPTS, LANES), 0) == iota((NPTS, LANES), 1) // WIDTH).astype(f32)
    for s in range(5):
        mat = coup[s] if s < 4 else stiff[...]
        cr[s] = lax.dot_general(
            mat, spread, (((0,), (0,)), ((), ())), precision=highest, preferred_element_type=f32
        )
    for h in range(2):
        w = swap_chunks(
            [jnp.broadcast_to(metric[h * 8 + q : h * 8 + q + 1, :], (8, 128)) for q in range(8)]
        )
        for b in range(BLOCKS):
            met[b, :, h * 128 : (h + 1) * 128] = w[b]
    own = jnp.concatenate([nbr[...], nbr[...]], axis=0) - first
    w = swap_chunks([own] * 8)
    for b in range(BLOCKS):
        near[b] = w[b] - b * WIDTH
    hi, lo = split(vert[...])
    vv[:LEV, :LEV] = hi
    vv[:LEV, LEV:] = hi
    vv[LEV:, :LEV] = lo
    vv[LEV:, LEV:] = jnp.zeros((LEV, LEV), bf16)


def operator_block(b, near, cr, th, tl):
    sub, lane = iota((WIDTH, LANES), 0), iota((WIDTH, LANES), 1)
    rows = near[b]
    inner, outer = [], []
    for s in range(4):
        r = rows[s : s + 1, :]
        r = jnp.concatenate([r, r], axis=1)
        hit = sub == jnp.broadcast_to(r & (WIDTH - 1), (WIDTH, LANES))
        inside = jnp.broadcast_to((r >= 0) & (r < WIDTH), (WIDTH, LANES))
        inner.append(hit & inside)
        outer.append(hit & jnp.logical_not(inside))
    diag = sub == (lane & (WIDTH - 1))
    for q in range(NPTS):
        vals = [jnp.broadcast_to(cr[s, q : q + 1, :], (WIDTH, LANES)) for s in range(5)]
        c = jnp.where(diag, vals[4], 0.0)
        d = jnp.zeros((WIDTH, LANES), f32)
        for s in range(4):
            c = c + jnp.where(inner[s], vals[s], 0.0)
            d = d + jnp.where(outer[s], vals[s], 0.0)
        for base, part in ((0, c), (LANES, d)):
            hi, lo = split(part)
            here = slice(base + q * WIDTH, base + (q + 1) * WIDTH)
            th[b, here, :] = hi
            tl[b, here, :] = lo


def advance(b, x, xh, xl, y, yh, yl, vv, th, tl, met):
    low = (iota((ROWS, LANES), 1) & (WIDTH - 1)) < WIDTH // 2
    sh = jnp.where(low, xh[b + 2], xh[b])
    sl = jnp.where(low, xl[b + 2], xl[b])
    ch, cl = xh[b + 1], xl[b + 1]
    lhs = jnp.concatenate([ch, sh, cl, sl, ch, sh], axis=1)
    rhs = jnp.concatenate([th[b], th[b], tl[b]], axis=0)
    acc = jnp.dot(lhs, rhs, preferred_element_type=f32)
    for f in range(FIELDS):
        g = slice(f * LEV, (f + 1) * LEV)
        parts = jnp.concatenate([xh[b + 1, g], xl[b + 1, g]], axis=0)
        v = jnp.dot(vv[...], parts, preferred_element_type=f32)
        new = x[b, g] + met[b, 0:1, :] * (acc[g] + v[:LEV] + v[LEV:])
        y[b, g] = new
        if yh is not None:
            hi, lo = split(new)
            yh[b + 1, g] = hi
            yl[b + 1, g] = lo


def add_surface(delta, y, yh, yl):
    last = iota((16, LANES), 0) == 15

    def body(b, _):
        for f in range(FIELDS):
            g = slice((f + 1) * LEV - 16, (f + 1) * LEV)
            new = y[b, g] + jnp.where(
                last, jnp.broadcast_to(delta[b, f : f + 1, :], (16, LANES)), 0.0
            )
            y[b, g] = new
            if yh is not None:
                hi, lo = split(new)
                yh[b + 1, g] = hi
                yl[b + 1, g] = lo
        return 0

    lax.fori_loop(0, BLOCKS, body, 0)


def edges_out(x, es):
    low = (iota((ROWS, 128), 1) & (WIDTH - 1)) < WIDTH // 2
    top = x[BLOCKS - 1]
    es[0] = jnp.where(low, pltpu.roll(top[:, 128:], 120, 1), top[:, :128])
    bottom = x[0]
    es[1] = jnp.where(low, bottom[:, :128], pltpu.roll(bottom[:, 128:], 8, 1))


def edges_in(er, xh, xl):
    for side, block, turn in ((0, 0, 8), (1, BLOCKS + 1, 120)):
        v = er[side]
        for cols, part in ((slice(0, 128), v), (slice(128, 256), pltpu.roll(v, turn, 1))):
            hi, lo = split(part)
            xh[block, :, cols] = hi
            xl[block, :, cols] = lo


def pair_tables(owner, block, src, slot_of, slot_to, point_of, point_to, ids):
    pair, col = iota((PAIRS, 256), 0), iota((PAIRS, 256), 1) // 8

    def over_columns(column):
        return jnp.sum(jnp.where(pair == col, column, 0.0), axis=0, keepdims=True)

    eye = iota((PAIRS, PAIRS), 0) == iota((PAIRS, PAIRS), 1)

    def as_column(row):
        wide = jnp.broadcast_to(row.astype(f32), (PAIRS, PAIRS))
        return jnp.sum(jnp.where(eye, wide, 0.0), axis=1, keepdims=True)

    own = jnp.broadcast_to(owner[...].astype(f32), (PAIRS, 256))
    own_c = over_columns(own)
    rank_c = jnp.sum(jnp.where((own == own_c) & (pair < col), 1.0, 0.0), axis=0, keepdims=True)
    slot_c = 2.0 * own_c + rank_c
    block_c = over_columns(jnp.broadcast_to(as_column(block[...]), (PAIRS, 256)))
    src_c = over_columns(jnp.broadcast_to(as_column(src[...]), (PAIRS, 256)))
    r, c = iota((256, 256), 0), iota((256, 256), 1)
    hit = ((r // 4).astype(f32) == slot_c) & ((r & 3) == (c & 7))
    table = hit.astype(f32)
    slot_of[...] = table.astype(bf16)
    slot_to[...] = table.T.astype(bf16)
    number = jnp.sum(table * (block_c + 1.0), axis=1, keepdims=True) - 1.0
    ids[...] = jnp.broadcast_to(number.astype(i32), (256, BLK)).reshape(DOM, 8, BLK)
    r, c = iota((64, 256), 0), iota((64, 256), 1)
    hit = ((r & 15).astype(f32) == src_c) & ((r // 16) == (c & 7))
    table = hit.astype(f32)
    point_of[...] = table.astype(bf16)
    point_to[...] = table.T.astype(bf16)


def pair_products(rows, wh, wl, out, transposed):
    dims = (((1,), (1 if transposed else 0,)), ((), ()))

    def body(i, _):
        for k in range(8):
            j = i * 8 + k
            v = rows[pl.ds(j * 8, 8), :]
            both = jnp.concatenate([v, v - v.astype(bf16).astype(f32)], axis=0).astype(bf16)
            a = lax.dot_general(both, wh[j], dims, preferred_element_type=f32)
            b = lax.dot_general(both, wl[j], dims, preferred_element_type=f32)
            out[pl.ds(j * 8, 8), :] = a[:8] + a[8:] + b[:8]
        return 0

    lax.fori_loop(0, PAIRS // 8, body, 0)


def kernel(
    state_hbm, weight_hbm, ocean_hbm, nbr, metric, coef, stiff, coup, vert,
    cell_nbr, cell_diff, overt, mask, owner, block, src,
    atm_hbm, ocean_out_hbm,
    st, x, xh, xl, y, yh, yl, vv, th, tl, met, cr, near, delta, flux,
    wt, wh, wl, rows_a, rows_b, slot_of, slot_to, point_of, point_to,
    es, er, es2, er2,
    ids_s, ids_r, rep_s, rep_r, flx_s, flx_r, surf_s, surf_r, ofl_s, ofl_r,
    oe, ob,
    st_sem, wt_sem, oc_sem, out_sem, zero_sem,
    ids_ss, ids_rs, rep_ss, rep_rs, flx_ss, flx_rs,
    surf_ss, surf_rs, ofl_ss, ofl_rs,
    edge_ss, edge_rs, edge2_ss, edge2_rs, oh_ss, oh_rs,
):
    c, d = lax.axis_index("comp"), lax.axis_index("dom")
    barrier = pltpu.get_barrier_semaphore()
    ocean_slab = SLABS - 1

    def remote(src_ref, dst_ref, send, recv, comp, dom):
        return pltpu.make_async_remote_copy(
            src_ref=src_ref, dst_ref=dst_ref, send_sem=send, recv_sem=recv,
            device_id=(comp, dom), device_id_type=MESH,
        )

    def greet(comp, dom):
        pl.semaphore_signal(barrier, inc=1, device_id=(comp, dom), device_id_type=MESH)

    @pl.when(c < ATM)
    def _atmosphere():
        state_in = [
            pltpu.make_async_copy(
                state_hbm.at[pl.ds(f * 2048, 2048)], st.at[pl.ds(f * 2048, 2048)], st_sem.at[f]
            )
            for f in range(FIELDS)
        ]
        for copy in state_in:
            copy.start()
        weights_in = pltpu.make_async_copy(weight_hbm, wt, wt_sem)
        weights_in.start()
        has_prev, has_next = (c + d) > 0, (c * DOM + d) < ATM * DOM - 1
        prev_c, prev_d = jnp.where(d == 0, c - 1, c), lax.rem(d + DOM - 1, DOM)
        next_c, next_d = jnp.where(d == DOM - 1, c + 1, c), lax.rem(d + 1, DOM)

        def other(i):
            return lax.rem(d + i, DOM)

        def hello(i, _):
            greet(c, other(i))
            return 0

        lax.fori_loop(1, DOM, hello, 0)
        greet(ocean_slab, d)
        cross_prev = (d == 0) & (c > 0)
        cross_next = (d == DOM - 1) & (c < ATM - 1)

        @pl.when(cross_prev)
        def _():
            greet(prev_c, prev_d)

        @pl.when(cross_next)
        def _():
            greet(next_c, next_d)

        pair_tables(owner, block, src, slot_of, slot_to, point_of, point_to, ids_s)
        pl.semaphore_wait(
            barrier, DOM + jnp.where(cross_prev, 1, 0) + jnp.where(cross_next, 1, 0)
        )

        def exchange(out, into, send, recv):
            def copy(i):
                o = other(i)
                return o, remote(out.at[o], into.at[d], send.at[o], recv.at[d], c, o)

            def start():
                def body(i, _):
                    copy(i)[1].start()
                    return 0

                into[d] = out[d]
                lax.fori_loop(1, DOM, body, 0)

            def arrive():
                def body(i, _):
                    o = other(i)
                    remote(out.at[o], into.at[o], send.at[o], recv.at[o], c, o).wait_recv()
                    return 0

                lax.fori_loop(1, DOM, body, 0)

            def sent():
                def body(i, _):
                    copy(i)[1].wait_send()
                    return 0

                lax.fori_loop(1, DOM, body, 0)

            return start, arrive, sent

        ids_start, ids_arrive, ids_sent = exchange(ids_s, ids_r, ids_ss, ids_rs)
        rep_start, rep_arrive, rep_sent = exchange(rep_s, rep_r, rep_ss, rep_rs)
        flx_start, flx_arrive, flx_sent = exchange(flx_s, flx_r, flx_ss, flx_rs)
        ids_start()

        def edge_copies(out, into, send, recv):
            up = remote(out.at[0], into.at[0], send.at[0], recv.at[0], next_c, next_d)
            down = remote(out.at[1], into.at[1], send.at[1], recv.at[1], prev_c, prev_d)

            def start():
                @pl.when(has_next)
                def _():
                    up.start()

                @pl.when(has_prev)
                def _():
                    down.start()

                @pl.when(jnp.logical_not(has_prev))
                def _():
                    into[0] = jnp.zeros((ROWS, 128), f32)

                @pl.when(jnp.logical_not(has_next))
                def _():
                    into[1] = jnp.zeros((ROWS, 128), f32)

            def arrive():
                @pl.when(has_prev)
                def _():
                    up.wait_recv()

                @pl.when(has_next)
                def _():
                    down.wait_recv()

            def sent():
                @pl.when(has_next)
                def _():
                    up.wait_send()

                @pl.when(has_prev)
                def _():
                    down.wait_send()

            return start, arrive, sent

        edge_start, edge_arrive, edge_sent = edge_copies(es, er, edge_ss, edge_rs)
        edge2_start, edge2_arrive, edge2_sent = edge_copies(es2, er2, edge2_ss, edge2_rs)

        for f in range(FIELDS):
            state_in[f].wait()
            pack(f, st, x, xh, xl)
        edges_out(x, es)
        edge_start()

        small_tables(c * (DOM * ELEMS) + d * ELEMS, nbr, metric, stiff, coup, vert, cr, met, near, vv)

        def table(b, _):
            operator_block(b, near, cr, th, tl)
            return 0

        lax.fori_loop(0, BLOCKS, table, 0)

        remote(surf_s, surf_r, surf_ss.at[0], surf_rs, ocean_slab, d).wait_recv()
        ids_arrive()

        def answer(i, _):
            which = ids_r[i]
            acc = jnp.zeros((8, BLK), f32)
            for b in range(OBLOCKS):
                acc = acc + jnp.where(which == b, surf_r[:, b * BLK : (b + 1) * BLK], 0.0)
            rep_s[i] = acc
            return 0

        lax.fori_loop(0, DOM, answer, 0, unroll=4)
        rep_start()

        weights_in.wait()

        def halves(j, _):
            hi, lo = split(wt[j])
            wh[j] = hi
            wl[j] = lo
            return 0

        lax.fori_loop(0, PAIRS, halves, 0, unroll=2)

        def first(i, _):
            @pl.when(i == BLOCKS - 2)
            def _():
                edge_arrive()
                edges_in(er, xh, xl)

            b = jnp.where(i < BLOCKS - 2, i + 1, (i - (BLOCKS - 2)) * (BLOCKS - 1))
            advance(b, x, xh, xl, y, yh, yl, vv, th, tl, met)
            return 0

        lax.fori_loop(0, BLOCKS, first, 0)

        rep_arrive()
        rows_a[...] = pick_rows(slot_to[...], rep_r[...].reshape(256, BLK))
        pair_products(rows_a, wh, wl, rows_b, True)
        surface = pick_rows(point_of[...], rows_b[...])
        top = jnp.concatenate(
            [st[f * 2048 + 2032 : f * 2048 + 2048, :] for f in range(FIELDS)], axis=0
        )
        fl = jnp.concatenate([coef[...]] * FIELDS, axis=0) * (top - surface)
        rows_a[...] = pick_rows(point_to[...], fl)
        pair_products(rows_a, wh, wl, rows_b, False)
        flx_s[...] = pick_rows(slot_of[...], rows_b[...]).reshape(DOM, 8, BLK)
        flx_start()

        flux[:64] = fl * -0.5
        flux[64:] = jnp.zeros((64, BLK), f32)
        for h in range(2):
            w = swap_chunks([flux[pl.ds(h * 8 + q, 8, stride=NPTS), :] for q in range(8)])
            for b in range(BLOCKS):
                delta[b, :, h * 128 : (h + 1) * 128] = w[b]
        add_surface(delta, y, yh, yl)
        edges_out(y, es2)
        edge2_start()

        def second(i, _):
            @pl.when(i == BLOCKS - 2)
            def _():
                edge2_arrive()
                edges_in(er2, yh, yl)
                flx_arrive()

                def gather(j, accs):
                    which, val = ids_r[j], flx_r[j]
                    return tuple(
                        acc + jnp.where(which == b, val, 0.0) for b, acc in enumerate(accs)
                    )

                zero = jnp.zeros((8, BLK), f32)
                accs = lax.fori_loop(0, DOM, gather, (zero,) * OBLOCKS, unroll=4)
                for b in range(OBLOCKS):
                    ofl_s[:, b * BLK : (b + 1) * BLK] = accs[b]
                remote(ofl_s, ofl_r.at[c], ofl_ss, ofl_rs.at[c], ocean_slab, d).start()

            b = jnp.where(i < BLOCKS - 2, i + 1, (i - (BLOCKS - 2)) * (BLOCKS - 1))
            advance(b, y, yh, yl, x, None, None, vv, th, tl, met)
            return 0

        lax.fori_loop(0, BLOCKS, second, 0)
        add_surface(delta, x, None, None)

        ob[...] = jnp.zeros((OROWS, CELLS), f32)
        zero_out = pltpu.make_async_copy(ob, ocean_out_hbm, zero_sem)
        zero_out.start()
        outs = [
            pltpu.make_async_copy(
                st.at[pl.ds(f * 2048, 2048)], atm_hbm.at[pl.ds(f * 2048, 2048)], out_sem.at[f]
            )
            for f in range(FIELDS)
        ]
        for f in range(FIELDS):
            unpack(f, x, st)
            outs[f].start()
        ids_sent()
        rep_sent()
        flx_sent()
        edge_sent()
        edge2_sent()
        remote(ofl_s, ofl_r.at[c], ofl_ss, ofl_rs.at[c], ocean_slab, d).wait_send()
        zero_out.wait()
        for copy in outs:
            copy.wait()

    @pl.when(c == ocean_slab)
    def _ocean():
        mid = oe.at[:, pl.ds(BLK, CELLS)]
        ocean_in = pltpu.make_async_copy(ocean_hbm, mid, oc_sem)
        ocean_in.start()
        for comp in range(ATM):
            greet(comp, d)
        has_prev, has_next = d > 0, d < DOM - 1

        @pl.when(has_prev)
        def _():
            greet(c, d - 1)

        @pl.when(has_next)
        def _():
            greet(c, d + 1)

        ocean_in.wait()
        for k in range(2):
            for f in range(FIELDS):
                surf_s[k * 4 + f : k * 4 + f + 1, :] = oe[f * OLEV : f * OLEV + 1, BLK : BLK + CELLS]
        pl.semaphore_wait(
            barrier, ATM + jnp.where(has_prev, 1, 0) + jnp.where(has_next, 1, 0)
        )
        surf_out = [
            remote(surf_s, surf_r, surf_ss.at[comp], surf_rs, comp, d) for comp in range(ATM)
        ]
        for copy in surf_out:
            copy.start()
        up = remote(
            oe.at[:, pl.ds(CELLS, BLK)], oe.at[:, pl.ds(0, BLK)],
            oh_ss.at[0], oh_rs.at[0], c, lax.rem(d + 1, DOM),
        )
        down = remote(
            oe.at[:, pl.ds(BLK, BLK)], oe.at[:, pl.ds(CELLS + BLK, BLK)],
            oh_ss.at[1], oh_rs.at[1], c, lax.rem(d + DOM - 1, DOM),
        )

        @pl.when(has_next)
        def _():
            up.start()

        @pl.when(has_prev)
        def _():
            down.start()

        st[...] = jnp.zeros((FIELDS * 2048, ELEMS), f32)
        zero_out = pltpu.make_async_copy(st, atm_hbm, zero_sem)
        zero_out.start()

        @pl.when(has_prev)
        def _():
            up.wait_recv()

        @pl.when(jnp.logical_not(has_prev))
        def _():
            oe[:, :BLK] = jnp.zeros((OROWS, BLK), f32)

        @pl.when(has_next)
        def _():
            down.wait_recv()

        @pl.when(jnp.logical_not(has_next))
        def _():
            oe[:, CELLS + BLK :] = jnp.zeros((OROWS, BLK), f32)

        source = iota((3 * BLK, BLK), 0)
        centre = source == iota((3 * BLK, BLK), 1) + BLK

        def cells(b, _):
            at = pl.multiple_of(b * BLK, BLK)
            here = pl.ds(at, BLK)
            rel = cell_nbr[:, here] - (d * CELLS + at - BLK)
            diff = cell_diff[:, here]
            total = jnp.sum(diff, axis=0, keepdims=True)
            mat = jnp.where(centre, jnp.broadcast_to(-total, (3 * BLK, BLK)), 0.0)
            for k in range(NBR_O):
                mat = mat + jnp.where(source == rel[k : k + 1, :], diff[k : k + 1, :], 0.0)
            lap = jnp.dot(
                oe[:, pl.ds(at, 3 * BLK)], mat, precision=highest, preferred_element_type=f32
            )
            for f in range(FIELDS):
                g = slice(f * OLEV, (f + 1) * OLEV)
                o = oe[g, pl.ds(at + BLK, BLK)]
                mix = jnp.dot(overt[...], o, precision=highest, preferred_element_type=f32)
                ob[g, here] = o + lap[g] + mix
            return 0

        lax.fori_loop(0, OBLOCKS, cells, 0)
        for comp in range(ATM):
            remote(ofl_s, ofl_r.at[comp], ofl_ss, ofl_rs.at[comp], comp, d).wait_recv()
        total = ofl_r[0] + ofl_r[1] + ofl_r[2]
        total = 0.5 * (total[:4] + total[4:])
        sea = mask[...] == 1
        first_row = iota((OLEV, CELLS), 0) == 0
        for f in range(FIELDS):
            g = slice(f * OLEV, (f + 1) * OLEV)
            fresh = ob[g, :] + jnp.where(first_row, total[f : f + 1, :], 0.0)
            ob[g, :] = jnp.where(sea, fresh, oe[g, BLK : BLK + CELLS])
        ocean_done = pltpu.make_async_copy(ob, ocean_out_hbm, out_sem.at[0])
        ocean_done.start()
        for copy in surf_out:
            copy.wait_send()

        @pl.when(has_next)
        def _():
            up.wait_send()

        @pl.when(has_prev)
        def _():
            down.wait_send()

        zero_out.wait()
        ocean_done.wait()


def local(
    atm_state, elem_nbr, elem_metric, bulk_coef, stiffness, coupling, atm_vertical,
    ocean_state, cell_nbr, cell_diff, ocean_vertical, sea_mask,
    pair_owner, pair_block, pair_src, remap_weight,
):
    vmem, sem = pltpu.VMEM, pltpu.SemaphoreType.DMA
    whole, anywhere = pl.BlockSpec(memory_space=pltpu.VMEM), pl.BlockSpec(memory_space=pl.ANY)
    big, halves = (BLOCKS, ROWS, LANES), (BLOCKS + 2, ROWS, LANES)
    message = (DOM, 8, BLK)
    scratch = [
        vmem((FIELDS * 2048, ELEMS), f32),
        vmem(big, f32), vmem(halves, bf16), vmem(halves, bf16),
        vmem(big, f32), vmem(halves, bf16), vmem(halves, bf16),
        vmem((2 * LEV, 2 * LEV), bf16), vmem((BLOCKS, 2 * LANES, LANES), bf16),
        vmem((BLOCKS, 2 * LANES, LANES), bf16), vmem((BLOCKS, 8, LANES), f32),
        vmem((5, NPTS, LANES), f32), vmem((BLOCKS, 8, 128), i32),
        vmem((BLOCKS, 8, LANES), f32), vmem((128, BLK), f32),
        vmem((PAIRS, BLK, BLK), f32), vmem((PAIRS, BLK, BLK), bf16), vmem((PAIRS, BLK, BLK), bf16),
        vmem((256, BLK), f32), vmem((256, BLK), f32),
        vmem((256, 256), bf16), vmem((256, 256), bf16), vmem((64, 256), bf16), vmem((256, 64), bf16),
        vmem((2, ROWS, 128), f32), vmem((2, ROWS, 128), f32),
        vmem((2, ROWS, 128), f32), vmem((2, ROWS, 128), f32),
        vmem(message, i32), vmem(message, i32), vmem(message, f32), vmem(message, f32),
        vmem(message, f32), vmem(message, f32),
        vmem((8, CELLS), f32), vmem((8, CELLS), f32), vmem((8, CELLS), f32),
        vmem((ATM, 8, CELLS), f32),
        vmem((OROWS, CELLS + 2 * BLK), f32), vmem((OROWS, CELLS), f32),
        sem((FIELDS,)), sem, sem, sem((FIELDS,)), sem,
        sem((DOM,)), sem((DOM,)), sem((DOM,)), sem((DOM,)), sem((DOM,)), sem((DOM,)),
        sem((ATM,)), sem, sem, sem((ATM,)),
        sem((2,)), sem((2,)), sem((2,)), sem((2,)), sem((2,)), sem((2,)),
    ]
    atm, ocean = pl.pallas_call(
        kernel,
        out_shape=(
            jax.ShapeDtypeStruct((FIELDS * 2048, ELEMS), f32),
            jax.ShapeDtypeStruct((OROWS, CELLS), f32),
        ),
        in_specs=[anywhere] * 3 + [whole] * 13,
        out_specs=(anywhere, anywhere),
        scratch_shapes=scratch,
        compiler_params=pltpu.CompilerParams(
            collective_id=0, has_side_effects=True, vmem_limit_bytes=60 << 20
        ),
        name="coupled_step",
    )(
        atm_state.reshape(FIELDS * 2048, ELEMS),
        remap_weight[0],
        ocean_state.reshape(OROWS, CELLS),
        elem_nbr[0], elem_metric[0], bulk_coef[0], stiffness, coupling, atm_vertical,
        cell_nbr[0], cell_diff[0], ocean_vertical, sea_mask,
        pair_owner[0], pair_block, pair_src,
    )
    return (
        atm.reshape(1, FIELDS, LEV, NPTS, ELEMS),
        ocean.reshape(1, FIELDS, OLEV, CELLS),
    )


def solution(mesh):
    in_specs = (
        P("comp", None, None, None, "dom"),
        P("comp", None, "dom"),
        P("comp", None, "dom"),
        P("comp", None, "dom"),
        P(),
        P(),
        P(),
        P("comp", None, None, "dom"),
        P("comp", None, "dom"),
        P("comp", None, "dom"),
        P(),
        P("comp", "dom"),
        P("comp", "dom", None),
        P("comp", "dom"),
        P("comp", "dom"),
        P("comp", "dom", None, None),
    )
    out_specs = (P("comp", None, None, None, "dom"), P("comp", None, None, "dom"))
    return jax.shard_map(local, mesh=mesh, in_specs=in_specs, out_specs=out_specs, check_vma=False)
```

```python
import functools

import jax
import jax.numpy as jnp
from jax import lax
from jax.experimental import pallas as pl
from jax.experimental.pallas import tpu as pltpu
from jax.sharding import PartitionSpec as P

f32, bf16, i32 = jnp.float32, jnp.bfloat16, jnp.int32
FIELDS, LEV, NPTS, ELEMS = 4, 128, 16, 128
ROWS = FIELDS * LEV
BLOCKS, WIDTH = 8, 16
LANES = NPTS * WIDTH
SLABS, DOM = 4, 32
ATM = SLABS - 1
PAIRS, BLK = 32, 128
OLEV, CELLS, NBR_O = 80, 1024, 6
OROWS = FIELDS * OLEV
OBLOCKS = CELLS // BLK
MESH = pl.DeviceIdType.MESH
highest = lax.Precision.HIGHEST


def iota(shape, axis):
    return lax.broadcasted_iota(i32, shape, axis)


def exchange_chunks(a):
    chunk = iota(a[0].shape, 1) // WIDTH
    for k in (1, 2, 4):
        take = (chunk & k) != 0
        a = [jnp.where(take, a[(i + k) % 8], a[i]) for i in range(8)]
    return [a[(-b) % 8] for b in range(8)]


def to_blocks(a):
    return exchange_chunks([a[q] if q == 0 else pltpu.roll(a[q], WIDTH * q, 1) for q in range(8)])


def from_blocks(a):
    a = exchange_chunks(a)
    return [a[q] if q == 0 else pltpu.roll(a[q], 128 - WIDTH * q, 1) for q in range(8)]


def split(x):
    hi = x.astype(bf16)
    return hi, (x - hi.astype(f32)).astype(bf16)


def pick_rows(onehot, x):
    hi, lo = split(x)
    return jnp.dot(onehot, hi, preferred_element_type=f32) + jnp.dot(
        onehot, lo, preferred_element_type=f32
    )


def pack(f, st, x, xh, xl):
    def body(i, _):
        row = f * LEV + i * 16
        for h in range(2):
            a = [st[pl.ds(row * NPTS + h * 8 + q, 16, stride=NPTS), :] for q in range(8)]
            w = to_blocks(a)
            cols = slice(h * 128, (h + 1) * 128)
            for b in range(BLOCKS):
                hi, lo = split(w[b])
                x[b, pl.ds(row, 16), cols] = w[b]
                xh[b + 1, pl.ds(row, 16), cols] = hi
                xl[b + 1, pl.ds(row, 16), cols] = lo
        return 0

    lax.fori_loop(0, LEV // 16, body, 0, unroll=2)


def unpack(f, x, st):
    def body(i, _):
        row = f * LEV + i * 16
        for h in range(2):
            cols = slice(h * 128, (h + 1) * 128)
            w = from_blocks([x[b, pl.ds(row, 16), cols] for b in range(BLOCKS)])
            for q in range(8):
                st[pl.ds(row * NPTS + h * 8 + q, 16, stride=NPTS), :] = w[q]
        return 0

    lax.fori_loop(0, LEV // 16, body, 0, unroll=2)


def small_tables(first, nbr, metric, stiff, coup, vert, cr, met, near, vv):
    spread = (iota((NPTS, LANES), 0) == iota((NPTS, LANES), 1) // WIDTH).astype(f32)
    for s in range(5):
        mat = coup[s] if s < 4 else stiff[...]
        cr[s] = lax.dot_general(
            mat, spread, (((0,), (0,)), ((), ())), precision=highest, preferred_element_type=f32
        )
    for h in range(2):
        w = to_blocks(
            [jnp.broadcast_to(metric[h * 8 + q : h * 8 + q + 1, :], (8, 128)) for q in range(8)]
        )
        for b in range(BLOCKS):
            met[b, :, h * 128 : (h + 1) * 128] = w[b]
    own = jnp.concatenate([nbr[...], nbr[...]], axis=0) - first
    w = to_blocks([own] * 8)
    for b in range(BLOCKS):
        near[b] = w[b] - b * WIDTH
    hi, lo = split(vert[...])
    vv[:LEV, :LEV] = hi
    vv[:LEV, LEV:] = hi
    vv[LEV:, :LEV] = lo
    vv[LEV:, LEV:] = jnp.zeros((LEV, LEV), bf16)


def operator_block(b, near, cr, turned, th, tl):
    sub, lane = iota((WIDTH, LANES), 0), iota((WIDTH, LANES), 1)
    for s in range(5):
        for h in range(2):
            cols = slice(h * 128, (h + 1) * 128)
            turned[s, :, cols] = pltpu.roll(cr[s, :, cols], b * WIDTH, 1)
    rows = near[b]
    inner, outer = [], []
    for s in range(4):
        r = rows[s : s + 1, :]
        r = jnp.concatenate([r, r], axis=1)
        hit = sub == jnp.broadcast_to(r & (WIDTH - 1), (WIDTH, LANES))
        inside = jnp.broadcast_to((r >= 0) & (r < WIDTH), (WIDTH, LANES))
        inner.append(hit & inside)
        outer.append(hit & jnp.logical_not(inside))
    diag = sub == (lane & (WIDTH - 1))
    half = (WIDTH // 2, LANES)

    def row(s, q, shape):
        return jnp.broadcast_to(turned[s, pl.ds(q, 1), :], shape)

    for k in range(NPTS):
        h, chunk = k - k % 8, k % 8
        q = h + ((chunk - b + 8) & 7)
        after = h + ((chunk - b + 7) & 7)
        before = h + ((chunk - b + 9) & 7)
        c = jnp.where(diag, row(4, q, (WIDTH, LANES)), 0.0)
        d = jnp.zeros((WIDTH, LANES), f32)
        for s in range(4):
            c = c + jnp.where(inner[s], row(s, q, (WIDTH, LANES)), 0.0)
            sides = jnp.concatenate([row(s, after, half), row(s, before, half)], axis=0)
            d = d + jnp.where(outer[s], sides, 0.0)
        for base, part in ((0, c), (LANES, d)):
            hi, lo = split(part)
            here = slice(base + k * WIDTH, base + (k + 1) * WIDTH)
            th[b, here, :] = hi
            tl[b, here, :] = lo


def advance(b, x, xh, xl, y, yh, yl, vv, th, tl, met):
    low = (iota((ROWS, LANES), 1) & (WIDTH - 1)) < WIDTH // 2
    sh = jnp.where(low, xh[b + 2], xh[b])
    sl = jnp.where(low, xl[b + 2], xl[b])
    ch, cl = xh[b + 1], xl[b + 1]
    lhs = jnp.concatenate([ch, sh, cl, sl, ch, sh], axis=1)
    rhs = jnp.concatenate([th[b], th[b], tl[b]], axis=0)
    acc = jnp.dot(lhs, rhs, preferred_element_type=f32)
    for f in range(FIELDS):
        g = slice(f * LEV, (f + 1) * LEV)
        parts = jnp.concatenate([xh[b + 1, g], xl[b + 1, g]], axis=0)
        v = jnp.dot(vv[...], parts, preferred_element_type=f32)
        new = x[b, g] + met[b, 0:1, :] * (acc[g] + v[:LEV] + v[LEV:])
        y[b, g] = new
        if yh is not None:
            hi, lo = split(new)
            yh[b + 1, g] = hi
            yl[b + 1, g] = lo


def add_surface(b, delta, y, yh, yl):
    last = iota((16, LANES), 0) == 15
    for f in range(FIELDS):
        g = slice((f + 1) * LEV - 16, (f + 1) * LEV)
        new = y[b, g] + jnp.where(last, jnp.broadcast_to(delta[b, f : f + 1, :], (16, LANES)), 0.0)
        y[b, g] = new
        if yh is not None:
            hi, lo = split(new)
            yh[b + 1, g] = hi
            yl[b + 1, g] = lo


def fold_edges(top, bottom):
    low = (iota((top.shape[0], 128), 1) & (WIDTH - 1)) < WIDTH // 2
    up = jnp.where(low, pltpu.roll(top[:, 128:], 120, 1), top[:, :128])
    down = jnp.where(low, bottom[:, :128], pltpu.roll(bottom[:, 128:], 8, 1))
    return up, down


def edges_out(f, x, es):
    g = slice(f * LEV, (f + 1) * LEV)
    es[0, g], es[1, g] = fold_edges(x[BLOCKS - 1, g], x[0, g])


def edges_in(er, xh, xl):
    for side, block, turn in ((0, 0, 8), (1, BLOCKS + 1, 120)):
        v = er[side]
        for cols, part in ((slice(0, 128), v), (slice(128, 256), pltpu.roll(v, turn, 1))):
            hi, lo = split(part)
            xh[block, :, cols] = hi
            xl[block, :, cols] = lo


def pair_tables(owner, block, src, slot_of, slot_to, point_of, point_to, ids):
    pair, col = iota((PAIRS, 256), 0), iota((PAIRS, 256), 1) // 8

    def over_columns(column):
        return jnp.sum(jnp.where(pair == col, column, 0.0), axis=0, keepdims=True)

    eye = iota((PAIRS, PAIRS), 0) == iota((PAIRS, PAIRS), 1)

    def as_column(row):
        wide = jnp.broadcast_to(row.astype(f32), (PAIRS, PAIRS))
        return jnp.sum(jnp.where(eye, wide, 0.0), axis=1, keepdims=True)

    own = jnp.broadcast_to(as_column(owner[...]), (PAIRS, 256))
    own_c = over_columns(own)
    rank_c = jnp.sum(jnp.where((own == own_c) & (pair < col), 1.0, 0.0), axis=0, keepdims=True)
    slot_c = 2.0 * own_c + rank_c
    block_c = over_columns(jnp.broadcast_to(as_column(block[...]), (PAIRS, 256)))
    src_c = over_columns(jnp.broadcast_to(as_column(src[...]), (PAIRS, 256)))
    r, c = iota((256, 256), 0), iota((256, 256), 1)
    hit = ((r // 4).astype(f32) == slot_c) & ((r & 3) == (c & 7))
    table = hit.astype(f32)
    slot_of[...] = table.astype(bf16)
    slot_to[...] = table.T.astype(bf16)
    number = jnp.sum(table * (block_c + 1.0), axis=1, keepdims=True) - 1.0
    ids[...] = jnp.broadcast_to(number.astype(i32), (256, BLK)).reshape(DOM, 8, BLK)
    r, c = iota((64, 256), 0), iota((64, 256), 1)
    hit = ((r & 15).astype(f32) == src_c) & ((r // 16) == (c & 7))
    table = hit.astype(f32)
    point_of[...] = table.astype(bf16)
    point_to[...] = table.T.astype(bf16)


def pair_products(rows, wh, wl, out, transposed):
    dims = (((1,), (1 if transposed else 0,)), ((), ()))

    def body(i, _):
        for k in range(16):
            j = i * 16 + k
            v = rows[pl.ds(j * 8, 8), :]
            both = jnp.concatenate([v, v - v.astype(bf16).astype(f32)], axis=0).astype(bf16)
            a = lax.dot_general(both, wh[j], dims, preferred_element_type=f32)
            b = lax.dot_general(both, wl[j], dims, preferred_element_type=f32)
            out[pl.ds(j * 8, 8), :] = a[:8] + a[8:] + b[:8]
        return 0

    lax.fori_loop(0, PAIRS // 16, body, 0)


def kernel(
    state_hbm, weight_hbm, ocean_hbm,
    nbr_h, metric_h, coef_h, stiff_h, coup_h, vert_h, owner_h, block_h, src_h,
    cell_nbr_h, cell_diff_h, overt_h, mask_h,
    packed_hbm, ocean_out_hbm,
    nbr, metric, coef, stiff, coup, vert, owner, block, src,
    cell_nbr, cell_diff, overt, mask,
    st, x, xh, xl, y, yh, yl, vv, th, tl, met, cr, turned, near, delta, flux,
    wt, wh, wl, rows_a, rows_b, slot_of, slot_to, point_of, point_to,
    es, er, es2, er2, es3, er3,
    ids_s, ids_r, rep_s, rep_r, flx_s, flx_r, surf_s, surf_r, ofl_s, ofl_r,
    oe, ob,
    small_sem, st_sem, wt_sem, oc_sem, out_sem,
    ids_ss, ids_rs, rep_ss, rep_rs, flx_ss, flx_rs,
    surf_ss, surf_rs, ofl_ss, ofl_rs,
    edge_ss, edge_rs, edge2_ss, edge2_rs, edge3_ss, edge3_rs, oh_ss, oh_rs,
):
    c, d = lax.axis_index("comp"), lax.axis_index("dom")
    barrier = pltpu.get_barrier_semaphore()
    ocean_slab = SLABS - 1

    def remote(src_ref, dst_ref, send, recv, comp, dom):
        return pltpu.make_async_remote_copy(
            src_ref=src_ref, dst_ref=dst_ref, send_sem=send, recv_sem=recv,
            device_id=(comp, dom), device_id_type=MESH,
        )

    def greet(comp, dom):
        pl.semaphore_signal(barrier, inc=1, device_id=(comp, dom), device_id_type=MESH)

    def fetch(pairs, first):
        copies = [
            pltpu.make_async_copy(a, b, small_sem.at[first + i]) for i, (a, b) in enumerate(pairs)
        ]
        for copy in copies:
            copy.start()
        return copies

    @pl.when(c < ATM)
    def _atmosphere():
        has_prev, has_next = (c + d) > 0, (c * DOM + d) < ATM * DOM - 1
        prev_c, prev_d = jnp.where(d == 0, c - 1, c), lax.rem(d + DOM - 1, DOM)
        next_c, next_d = jnp.where(d == DOM - 1, c + 1, c), lax.rem(d + 1, DOM)
        cross_prev = (d == 0) & (c > 0)
        cross_next = (d == DOM - 1) & (c < ATM - 1)

        def other(i):
            return lax.rem(d + i, DOM)

        def hello(i, _):
            greet(c, other(i))
            return 0

        state_in = [
            pltpu.make_async_copy(
                state_hbm.at[pl.ds(f * 2048, 2048)], st.at[pl.ds(f * 2048, 2048)], st_sem.at[f]
            )
            for f in range(FIELDS)
        ]
        state_in[0].start()
        lax.fori_loop(1, DOM, hello, 0)
        greet(ocean_slab, d)

        @pl.when(cross_prev)
        def _():
            greet(prev_c, prev_d)

        @pl.when(cross_next)
        def _():
            greet(next_c, next_d)

        for copy in state_in[1:]:
            copy.start()
        small_in = fetch(
            [(owner_h, owner), (block_h, block), (src_h, src), (nbr_h, nbr), (metric_h, metric),
             (coef_h, coef), (stiff_h, stiff), (coup_h, coup), (vert_h, vert)], 0,
        )
        weights_in = pltpu.make_async_copy(weight_hbm, wt, wt_sem)
        weights_in.start()

        def exchange(out, into, send, recv):
            def copy(i):
                o = other(i)
                return o, remote(out.at[o], into.at[d], send.at[o], recv.at[d], c, o)

            def start():
                def body(i, _):
                    copy(i)[1].start()
                    return 0

                into[d] = out[d]
                lax.fori_loop(1, DOM, body, 0)

            def arrive():
                def body(i, _):
                    o = other(i)
                    remote(out.at[o], into.at[o], send.at[o], recv.at[o], c, o).wait_recv()
                    return 0

                lax.fori_loop(1, DOM, body, 0)

            def sent():
                def body(i, _):
                    copy(i)[1].wait_send()
                    return 0

                lax.fori_loop(1, DOM, body, 0)

            return start, arrive, sent

        ids_start, ids_arrive, ids_sent = exchange(ids_s, ids_r, ids_ss, ids_rs)
        rep_start, rep_arrive, rep_sent = exchange(rep_s, rep_r, rep_ss, rep_rs)
        flx_start, flx_arrive, flx_sent = exchange(flx_s, flx_r, flx_ss, flx_rs)

        def edge_copies(out, into, send, recv, rows):
            up = remote(out.at[0, rows], into.at[0, rows], send.at[0], recv.at[0], next_c, next_d)
            down = remote(out.at[1, rows], into.at[1, rows], send.at[1], recv.at[1], prev_c, prev_d)

            def start():
                @pl.when(has_next)
                def _():
                    up.start()

                @pl.when(has_prev)
                def _():
                    down.start()

            def arrive():
                @pl.when(has_prev)
                def _():
                    up.wait_recv()

                @pl.when(has_next)
                def _():
                    down.wait_recv()

            def sent():
                @pl.when(has_next)
                def _():
                    up.wait_send()

                @pl.when(has_prev)
                def _():
                    down.wait_send()

            return start, arrive, sent

        edges = [
            edge_copies(es, er, edge_ss.at[f], edge_rs.at[f], pl.ds(f * LEV, LEV))
            for f in range(FIELDS)
        ]
        edge2_start, edge2_arrive, edge2_sent = edge_copies(
            es2, er2, edge2_ss, edge2_rs, pl.ds(0, ROWS)
        )
        edge3_start, edge3_arrive, edge3_sent = edge_copies(
            es3, er3, edge3_ss, edge3_rs, pl.ds(0, 8)
        )

        @pl.when(jnp.logical_not(has_prev))
        def _():
            er[0] = jnp.zeros((ROWS, 128), f32)
            er2[0] = jnp.zeros((ROWS, 128), f32)
            er3[0] = jnp.zeros((8, 128), f32)

        @pl.when(jnp.logical_not(has_next))
        def _():
            er[1] = jnp.zeros((ROWS, 128), f32)
            er2[1] = jnp.zeros((ROWS, 128), f32)
            er3[1] = jnp.zeros((8, 128), f32)

        state_in[0].wait()
        pack(0, st, x, xh, xl)
        edges_out(0, x, es)
        for copy in small_in:
            copy.wait()
        pair_tables(owner, block, src, slot_of, slot_to, point_of, point_to, ids_s)
        pl.semaphore_wait(
            barrier, DOM + jnp.where(cross_prev, 1, 0) + jnp.where(cross_next, 1, 0)
        )
        edges[0][0]()
        ids_start()
        for f in range(1, FIELDS):
            state_in[f].wait()
            pack(f, st, x, xh, xl)
            edges_out(f, x, es)
            edges[f][0]()

        small_tables(c * (DOM * ELEMS) + d * ELEMS, nbr, metric, stiff, coup, vert, cr, met, near, vv)

        def table(b, _):
            operator_block(b, near, cr, turned, th, tl)
            return 0

        lax.fori_loop(0, BLOCKS, table, 0)

        remote(surf_s, surf_r, surf_ss.at[0], surf_rs, ocean_slab, d).wait_recv()
        ids_arrive()

        def answer(i, _):
            which = ids_r[i]
            acc = jnp.zeros((8, BLK), f32)
            for b in range(OBLOCKS):
                acc = acc + jnp.where(which == b, surf_r[:, b * BLK : (b + 1) * BLK], 0.0)
            rep_s[i] = acc
            return 0

        lax.fori_loop(0, DOM, answer, 0, unroll=4)
        rep_start()

        weights_in.wait()

        def halves(j, _):
            hi, lo = split(wt[j])
            wh[j] = hi
            wl[j] = lo
            return 0

        lax.fori_loop(0, PAIRS, halves, 0, unroll=2)

        def first(i, _):
            @pl.when(i == 4)
            def _():
                for f in range(FIELDS):
                    edges[f][1]()
                edges_in(er, xh, xl)

            @pl.when(i == 6)
            def _():
                for f in range(FIELDS):
                    edges_out(f, y, es2)
                edge2_start()

            edge = jnp.where(i == 4, 0, BLOCKS - 1)
            b = jnp.where(i < 4, i + 1, jnp.where(i < 6, edge, i - 1))
            advance(b, x, xh, xl, y, yh, yl, vv, th, tl, met)
            return 0

        lax.fori_loop(0, BLOCKS, first, 0)

        rep_arrive()
        rows_a[...] = pick_rows(slot_to[...], rep_r[...].reshape(256, BLK))
        pair_products(rows_a, wh, wl, rows_b, True)
        surface = pick_rows(point_of[...], rows_b[...])
        top = jnp.concatenate(
            [st[f * 2048 + 2032 : f * 2048 + 2048, :] for f in range(FIELDS)], axis=0
        )
        fl = jnp.concatenate([coef[...]] * FIELDS, axis=0) * (top - surface)
        rows_a[...] = pick_rows(point_to[...], fl)
        pair_products(rows_a, wh, wl, rows_b, False)
        flx_s[...] = pick_rows(slot_of[...], rows_b[...]).reshape(DOM, 8, BLK)
        flx_start()

        flux[:64] = fl * -0.5
        flux[64:] = jnp.zeros((64, BLK), f32)
        for h in range(2):
            w = to_blocks([flux[pl.ds(h * 8 + q, 8, stride=NPTS), :] for q in range(8)])
            for b in range(BLOCKS):
                delta[b, :, h * 128 : (h + 1) * 128] = w[b]
        es3[0], es3[1] = fold_edges(delta[BLOCKS - 1], delta[0])
        edge3_start()

        def surface_term(b, _):
            add_surface(b, delta, y, yh, yl)
            return 0

        lax.fori_loop(0, BLOCKS, surface_term, 0)

        def block_out(b):
            return pltpu.make_async_copy(x.at[b], packed_hbm.at[b], out_sem.at[b])

        def second(i, _):
            @pl.when(i == 3)
            def _():
                flx_arrive()

                def gather(j, accs):
                    which, val = ids_r[j], flx_r[j]
                    return tuple(
                        acc + jnp.where(which == b, val, 0.0) for b, acc in enumerate(accs)
                    )

                zero = jnp.zeros((8, BLK), f32)
                accs = lax.fori_loop(0, DOM, gather, (zero,) * OBLOCKS, unroll=4)
                for b in range(OBLOCKS):
                    ofl_s[:, b * BLK : (b + 1) * BLK] = accs[b]
                remote(ofl_s, ofl_r.at[c], ofl_ss, ofl_rs.at[c], ocean_slab, d).start()

            @pl.when(i == BLOCKS - 2)
            def _():
                edge2_arrive()
                edge3_arrive()
                last = iota((16, 128), 0) == 15
                for side in range(2):
                    for f in range(FIELDS):
                        g = slice((f + 1) * LEV - 16, (f + 1) * LEV)
                        extra = jnp.broadcast_to(er3[side, f : f + 1, :], (16, 128))
                        er2[side, g] = er2[side, g] + jnp.where(last, extra, 0.0)
                edges_in(er2, yh, yl)

            b = jnp.where(i < BLOCKS - 2, i + 1, (i - (BLOCKS - 2)) * (BLOCKS - 1))
            advance(b, y, yh, yl, x, None, None, vv, th, tl, met)
            add_surface(b, delta, x, None, None)
            block_out(b).start()
            return 0

        lax.fori_loop(0, BLOCKS, second, 0)
        ids_sent()
        rep_sent()
        flx_sent()
        for f in range(FIELDS):
            edges[f][2]()
        edge2_sent()
        edge3_sent()
        remote(ofl_s, ofl_r.at[c], ofl_ss, ofl_rs.at[c], ocean_slab, d).wait_send()
        for b in range(BLOCKS):
            block_out(b).wait()

    @pl.when(c == ocean_slab)
    def _ocean():
        mid = oe.at[:, pl.ds(BLK, CELLS)]
        ocean_in = pltpu.make_async_copy(ocean_hbm, mid, oc_sem)
        ocean_in.start()
        small_in = fetch(
            [(cell_nbr_h, cell_nbr), (cell_diff_h, cell_diff), (overt_h, overt), (mask_h, mask)], 0
        )
        for comp in range(ATM):
            greet(comp, d)
        has_prev, has_next = d > 0, d < DOM - 1

        @pl.when(has_prev)
        def _():
            greet(c, d - 1)

        @pl.when(has_next)
        def _():
            greet(c, d + 1)

        ocean_in.wait()
        for k in range(2):
            for f in range(FIELDS):
                surf_s[k * 4 + f : k * 4 + f + 1, :] = oe[f * OLEV : f * OLEV + 1, BLK : BLK + CELLS]
        pl.semaphore_wait(
            barrier, ATM + jnp.where(has_prev, 1, 0) + jnp.where(has_next, 1, 0)
        )
        surf_out = [
            remote(surf_s, surf_r, surf_ss.at[comp], surf_rs, comp, d) for comp in range(ATM)
        ]
        for copy in surf_out:
            copy.start()
        up = remote(
            oe.at[:, pl.ds(CELLS, BLK)], oe.at[:, pl.ds(0, BLK)],
            oh_ss.at[0], oh_rs.at[0], c, lax.rem(d + 1, DOM),
        )
        down = remote(
            oe.at[:, pl.ds(BLK, BLK)], oe.at[:, pl.ds(CELLS + BLK, BLK)],
            oh_ss.at[1], oh_rs.at[1], c, lax.rem(d + DOM - 1, DOM),
        )

        @pl.when(has_next)
        def _():
            up.start()

        @pl.when(has_prev)
        def _():
            down.start()

        @pl.when(has_prev)
        def _():
            up.wait_recv()

        @pl.when(jnp.logical_not(has_prev))
        def _():
            oe[:, :BLK] = jnp.zeros((OROWS, BLK), f32)

        @pl.when(has_next)
        def _():
            down.wait_recv()

        @pl.when(jnp.logical_not(has_next))
        def _():
            oe[:, CELLS + BLK :] = jnp.zeros((OROWS, BLK), f32)

        for copy in small_in:
            copy.wait()
        source = iota((3 * BLK, BLK), 0)
        centre = source == iota((3 * BLK, BLK), 1) + BLK

        def cells(b, _):
            at = pl.multiple_of(b * BLK, BLK)
            here = pl.ds(at, BLK)
            rel = [cell_nbr[k, :, here] - (d * CELLS + at - BLK) for k in range(NBR_O)]
            diff = [cell_diff[k, :, here] for k in range(NBR_O)]
            mat = jnp.where(centre, jnp.broadcast_to(-sum(diff), (3 * BLK, BLK)), 0.0)
            for k in range(NBR_O):
                mat = mat + jnp.where(source == rel[k], diff[k], 0.0)
            lap = jnp.dot(
                oe[:, pl.ds(at, 3 * BLK)], mat, precision=highest, preferred_element_type=f32
            )
            for f in range(FIELDS):
                g = slice(f * OLEV, (f + 1) * OLEV)
                o = oe[g, pl.ds(at + BLK, BLK)]
                mix = jnp.dot(overt[...], o, precision=highest, preferred_element_type=f32)
                ob[g, here] = o + lap[g] + mix
            return 0

        lax.fori_loop(0, OBLOCKS, cells, 0)
        for comp in range(ATM):
            remote(ofl_s, ofl_r.at[comp], ofl_ss, ofl_rs.at[comp], comp, d).wait_recv()
        total = ofl_r[0] + ofl_r[1] + ofl_r[2]
        total = 0.5 * (total[:4] + total[4:])
        sea = mask[...] == 1
        first_row = iota((OLEV, CELLS), 0) == 0
        for f in range(FIELDS):
            g = slice(f * OLEV, (f + 1) * OLEV)
            fresh = ob[g, :] + jnp.where(first_row, total[f : f + 1, :], 0.0)
            ob[g, :] = jnp.where(sea, fresh, oe[g, BLK : BLK + CELLS])
        ocean_done = pltpu.make_async_copy(ob, ocean_out_hbm, out_sem.at[0])
        ocean_done.start()
        for copy in surf_out:
            copy.wait_send()

        @pl.when(has_next)
        def _():
            up.wait_send()

        @pl.when(has_prev)
        def _():
            down.wait_send()

        ocean_done.wait()


def finish(packed_hbm, ocean_hbm, atm_hbm, ocean_out_hbm, x, st, blank, in_sem, out_sem, oc_sem):
    c = lax.axis_index("comp")
    outs = [
        pltpu.make_async_copy(
            st.at[pl.ds(f * 2048, 2048)], atm_hbm.at[pl.ds(f * 2048, 2048)], out_sem.at[f]
        )
        for f in range(FIELDS)
    ]

    @pl.when(c < ATM)
    def _():
        ins = [
            pltpu.make_async_copy(
                packed_hbm.at[:, pl.ds(f * LEV, LEV)], x.at[:, pl.ds(f * LEV, LEV)], in_sem.at[f]
            )
            for f in range(FIELDS)
        ]
        for copy in ins:
            copy.start()
        blank[...] = jnp.zeros((OROWS, CELLS), f32)
        zero_out = pltpu.make_async_copy(blank, ocean_out_hbm, oc_sem)
        zero_out.start()
        for f in range(FIELDS):
            ins[f].wait()
            unpack(f, x, st)
            outs[f].start()
        zero_out.wait()
        for copy in outs:
            copy.wait()

    @pl.when(c == ATM)
    def _():
        ocean_out = pltpu.make_async_copy(ocean_hbm, ocean_out_hbm, oc_sem)
        ocean_out.start()
        for f in range(FIELDS):
            st[f * 2048 : (f + 1) * 2048] = jnp.zeros((2048, ELEMS), f32)
            outs[f].start()
        ocean_out.wait()
        for copy in outs:
            copy.wait()


def local(
    atm_state, elem_nbr, elem_metric, bulk_coef, stiffness, coupling, atm_vertical,
    ocean_state, cell_nbr, cell_diff, ocean_vertical, sea_mask,
    pair_owner, pair_block, pair_src, remap_weight,
):
    vmem, sem = pltpu.VMEM, pltpu.SemaphoreType.DMA
    anywhere = pl.BlockSpec(memory_space=pl.ANY)
    big, halves = (BLOCKS, ROWS, LANES), (BLOCKS + 2, ROWS, LANES)
    message = (DOM, 8, BLK)
    scratch = [
        vmem((4, ELEMS), i32), vmem((NPTS, ELEMS), f32), vmem((NPTS, ELEMS), f32),
        vmem((NPTS, NPTS), f32), vmem((4, NPTS, NPTS), f32), vmem((LEV, LEV), f32),
        vmem((1, PAIRS), i32), vmem((1, PAIRS), i32), vmem((1, PAIRS), i32),
        vmem((NBR_O, 1, CELLS), i32), vmem((NBR_O, 1, CELLS), f32), vmem((OLEV, OLEV), f32),
        vmem((1, CELLS), i32),
        vmem((FIELDS * 2048, ELEMS), f32),
        vmem(big, f32), vmem(halves, bf16), vmem(halves, bf16),
        vmem(big, f32), vmem(halves, bf16), vmem(halves, bf16),
        vmem((2 * LEV, 2 * LEV), bf16), vmem((BLOCKS, 2 * LANES, LANES), bf16),
        vmem((BLOCKS, 2 * LANES, LANES), bf16), vmem((BLOCKS, 8, LANES), f32),
        vmem((5, NPTS, LANES), f32), vmem((5, NPTS, LANES), f32), vmem((BLOCKS, 8, 128), i32),
        vmem((BLOCKS, 8, LANES), f32), vmem((128, BLK), f32),
        vmem((PAIRS, BLK, BLK), f32), vmem((PAIRS, BLK, BLK), bf16), vmem((PAIRS, BLK, BLK), bf16),
        vmem((256, BLK), f32), vmem((256, BLK), f32),
        vmem((256, 256), bf16), vmem((256, 256), bf16), vmem((64, 256), bf16), vmem((256, 64), bf16),
        vmem((2, ROWS, 128), f32), vmem((2, ROWS, 128), f32),
        vmem((2, ROWS, 128), f32), vmem((2, ROWS, 128), f32),
        vmem((2, 8, 128), f32), vmem((2, 8, 128), f32),
        vmem(message, i32), vmem(message, i32), vmem(message, f32), vmem(message, f32),
        vmem(message, f32), vmem(message, f32),
        vmem((8, CELLS), f32), vmem((8, CELLS), f32), vmem((8, CELLS), f32),
        vmem((ATM, 8, CELLS), f32),
        vmem((OROWS, CELLS + 2 * BLK), f32), vmem((OROWS, CELLS), f32),
        sem((9,)), sem((FIELDS,)), sem, sem, sem((BLOCKS,)),
        sem((DOM,)), sem((DOM,)), sem((DOM,)), sem((DOM,)), sem((DOM,)), sem((DOM,)),
        sem((ATM,)), sem, sem, sem((ATM,)),
        sem((FIELDS, 2)), sem((FIELDS, 2)), sem((2,)), sem((2,)), sem((2,)), sem((2,)),
        sem((2,)), sem((2,)),
    ]
    packed, ocean = pl.pallas_call(
        kernel,
        out_shape=(jax.ShapeDtypeStruct(big, f32), jax.ShapeDtypeStruct((OROWS, CELLS), f32)),
        in_specs=[anywhere] * 16,
        out_specs=(anywhere, anywhere),
        scratch_shapes=scratch,
        compiler_params=pltpu.CompilerParams(
            collective_id=0, has_side_effects=True, vmem_limit_bytes=60 << 20
        ),
        name="coupled_step",
    )(
        atm_state.reshape(FIELDS * 2048, ELEMS),
        remap_weight[0],
        ocean_state.reshape(OROWS, CELLS),
        elem_nbr[0], elem_metric[0], bulk_coef[0], stiffness, coupling, atm_vertical,
        pair_owner.reshape(1, PAIRS), pair_block, pair_src,
        jnp.transpose(cell_nbr, (1, 0, 2)), jnp.transpose(cell_diff, (1, 0, 2)),
        ocean_vertical, sea_mask,
    )
    atm, ocean = pl.pallas_call(
        finish,
        out_shape=(
            jax.ShapeDtypeStruct((FIELDS * 2048, ELEMS), f32),
            jax.ShapeDtypeStruct((OROWS, CELLS), f32),
        ),
        in_specs=[anywhere] * 2,
        out_specs=(anywhere, anywhere),
        scratch_shapes=[
            vmem(big, f32), vmem((FIELDS * 2048, ELEMS), f32), vmem((OROWS, CELLS), f32),
            sem((FIELDS,)), sem((FIELDS,)), sem,
        ],
        compiler_params=pltpu.CompilerParams(vmem_limit_bytes=60 << 20),
        name="finish",
    )(packed, ocean)
    return (
        atm.reshape(1, FIELDS, LEV, NPTS, ELEMS),
        ocean.reshape(1, FIELDS, OLEV, CELLS),
    )


def solution(mesh):
    in_specs = (
        P("comp", None, None, None, "dom"),
        P("comp", None, "dom"),
        P("comp", None, "dom"),
        P("comp", None, "dom"),
        P(),
        P(),
        P(),
        P("comp", None, None, "dom"),
        P("comp", None, "dom"),
        P("comp", None, "dom"),
        P(),
        P("comp", "dom"),
        P("comp", "dom", None),
        P("comp", "dom"),
        P("comp", "dom"),
        P("comp", "dom", None, None),
    )
    out_specs = (P("comp", None, None, None, "dom"), P("comp", None, None, "dom"))
    return jax.shard_map(local, mesh=mesh, in_specs=in_specs, out_specs=out_specs, check_vma=False)
```

```python
import functools

import jax
import jax.numpy as jnp
from jax import lax
from jax.experimental import pallas as pl
from jax.experimental.pallas import tpu as pltpu
from jax.sharding import PartitionSpec as P

f32, bf16, i32 = jnp.float32, jnp.bfloat16, jnp.int32
FIELDS, LEV, NPTS, ELEMS = 4, 128, 16, 128
ROWS = FIELDS * LEV
BLOCKS, WIDTH = 8, 16
LANES = NPTS * WIDTH
SLABS, DOM = 4, 32
ATM = SLABS - 1
PAIRS, BLK = 32, 128
OLEV, CELLS, NBR_O = 80, 1024, 6
OROWS = FIELDS * OLEV
OBLOCKS = CELLS // BLK
MESH = pl.DeviceIdType.MESH
highest = lax.Precision.HIGHEST


def iota(shape, axis):
    return lax.broadcasted_iota(i32, shape, axis)


def exchange_chunks(a):
    chunk = iota(a[0].shape, 1) // WIDTH
    for k in (1, 2, 4):
        take = (chunk & k) != 0
        a = [jnp.where(take, a[(i + k) % 8], a[i]) for i in range(8)]
    return [a[(-b) % 8] for b in range(8)]


def to_blocks(a):
    return exchange_chunks([a[q] if q == 0 else pltpu.roll(a[q], WIDTH * q, 1) for q in range(8)])


def from_blocks(a):
    a = exchange_chunks(a)
    return [a[q] if q == 0 else pltpu.roll(a[q], 128 - WIDTH * q, 1) for q in range(8)]


def split(x):
    hi = x.astype(bf16)
    return hi, (x - hi.astype(f32)).astype(bf16)


def pick_rows(onehot, x):
    hi, lo = split(x)
    return jnp.dot(onehot, hi, preferred_element_type=f32) + jnp.dot(
        onehot, lo, preferred_element_type=f32
    )


def pack(f, st, x, xh, xl):
    def body(i, _):
        row = f * LEV + i * 16
        for h in range(2):
            a = [st[pl.ds(row * NPTS + h * 8 + q, 16, stride=NPTS), :] for q in range(8)]
            w = to_blocks(a)
            cols = slice(h * 128, (h + 1) * 128)
            for b in range(BLOCKS):
                hi, lo = split(w[b])
                x[b, pl.ds(row, 16), cols] = w[b]
                xh[b + 1, pl.ds(row, 16), cols] = hi
                xl[b + 1, pl.ds(row, 16), cols] = lo
        return 0

    lax.fori_loop(0, LEV // 16, body, 0, unroll=2)


def unpack(first, levels, x, st):
    def body(i, _):
        row = first + i * 16
        for h in range(2):
            cols = slice(h * 128, (h + 1) * 128)
            w = from_blocks([x[b, pl.ds(row, 16), cols] for b in range(BLOCKS)])
            for q in range(8):
                st[pl.ds(row * NPTS + h * 8 + q, 16, stride=NPTS), :] = w[q]
        return 0

    lax.fori_loop(0, levels // 16, body, 0, unroll=2)


def small_tables(first, nbr, metric, stiff, coup, vert, cr, met, near, vv):
    spread = (iota((NPTS, LANES), 0) == iota((NPTS, LANES), 1) // WIDTH).astype(f32)
    for s in range(5):
        mat = coup[s] if s < 4 else stiff[...]
        cr[s] = lax.dot_general(
            mat, spread, (((0,), (0,)), ((), ())), precision=highest, preferred_element_type=f32
        )
    for h in range(2):
        w = to_blocks(
            [jnp.broadcast_to(metric[h * 8 + q : h * 8 + q + 1, :], (8, 128)) for q in range(8)]
        )
        for b in range(BLOCKS):
            met[b, :, h * 128 : (h + 1) * 128] = w[b]
    own = jnp.concatenate([nbr[...], nbr[...]], axis=0) - first
    w = to_blocks([own] * 8)
    for b in range(BLOCKS):
        near[b] = w[b] - b * WIDTH
    hi, lo = split(vert[...])
    vv[:LEV, :LEV] = hi
    vv[:LEV, LEV:] = hi
    vv[LEV:, :LEV] = lo
    vv[LEV:, LEV:] = jnp.zeros((LEV, LEV), bf16)


def operator_block(b, near, cr, turned, th, tl):
    sub, lane = iota((WIDTH, LANES), 0), iota((WIDTH, LANES), 1)
    for s in range(5):
        for h in range(2):
            cols = slice(h * 128, (h + 1) * 128)
            turned[s, :, cols] = pltpu.roll(cr[s, :, cols], b * WIDTH, 1)
    rows = near[b]
    inner, outer = [], []
    for s in range(4):
        r = rows[s : s + 1, :]
        r = jnp.concatenate([r, r], axis=1)
        hit = sub == jnp.broadcast_to(r & (WIDTH - 1), (WIDTH, LANES))
        inside = jnp.broadcast_to((r >= 0) & (r < WIDTH), (WIDTH, LANES))
        inner.append(hit & inside)
        outer.append(hit & jnp.logical_not(inside))
    diag = sub == (lane & (WIDTH - 1))
    half = (WIDTH // 2, LANES)

    def row(s, q, shape):
        return jnp.broadcast_to(turned[s, pl.ds(q, 1), :], shape)

    for k in range(NPTS):
        h, chunk = k - k % 8, k % 8
        q = h + ((chunk - b + 8) & 7)
        after = h + ((chunk - b + 7) & 7)
        before = h + ((chunk - b + 9) & 7)
        c = jnp.where(diag, row(4, q, (WIDTH, LANES)), 0.0)
        d = jnp.zeros((WIDTH, LANES), f32)
        for s in range(4):
            c = c + jnp.where(inner[s], row(s, q, (WIDTH, LANES)), 0.0)
            sides = jnp.concatenate([row(s, after, half), row(s, before, half)], axis=0)
            d = d + jnp.where(outer[s], sides, 0.0)
        for base, part in ((0, c), (LANES, d)):
            hi, lo = split(part)
            here = slice(base + k * WIDTH, base + (k + 1) * WIDTH)
            th[b, here, :] = hi
            tl[b, here, :] = lo


def advance(b, x, xh, xl, y, yh, yl, vv, th, tl, met, delta=None):
    last = iota((16, LANES), 0) == 15
    low = (iota((ROWS, LANES), 1) & (WIDTH - 1)) < WIDTH // 2
    sh = jnp.where(low, xh[b + 2], xh[b])
    sl = jnp.where(low, xl[b + 2], xl[b])
    ch, cl = xh[b + 1], xl[b + 1]
    lhs = jnp.concatenate([ch, sh, cl, sl, ch, sh], axis=1)
    rhs = jnp.concatenate([th[b], th[b], tl[b]], axis=0)
    acc = jnp.dot(lhs, rhs, preferred_element_type=f32)
    for f in range(FIELDS):
        g = slice(f * LEV, (f + 1) * LEV)
        parts = jnp.concatenate([xh[b + 1, g], xl[b + 1, g]], axis=0)
        v = jnp.dot(vv[...], parts, preferred_element_type=f32)
        new = x[b, g] + met[b, 0:1, :] * (acc[g] + v[:LEV] + v[LEV:])
        if delta is not None:
            extra = jnp.broadcast_to(delta[b, f : f + 1, :], (16, LANES))
            tail = new[LEV - 16 :] + jnp.where(last, extra, 0.0)
            new = jnp.concatenate([new[: LEV - 16], tail], axis=0)
        y[b, g] = new
        if yh is not None:
            hi, lo = split(new)
            yh[b + 1, g] = hi
            yl[b + 1, g] = lo


def add_surface(b, delta, y, yh, yl):
    last = iota((16, LANES), 0) == 15
    for f in range(FIELDS):
        g = slice((f + 1) * LEV - 16, (f + 1) * LEV)
        new = y[b, g] + jnp.where(last, jnp.broadcast_to(delta[b, f : f + 1, :], (16, LANES)), 0.0)
        y[b, g] = new
        hi, lo = split(new)
        yh[b + 1, g] = hi
        yl[b + 1, g] = lo


def fold_edges(top, bottom):
    low = (iota((top.shape[0], 128), 1) & (WIDTH - 1)) < WIDTH // 2
    up = jnp.where(low, pltpu.roll(top[:, 128:], 120, 1), top[:, :128])
    down = jnp.where(low, bottom[:, :128], pltpu.roll(bottom[:, 128:], 8, 1))
    return up, down


def edges_out(f, x, es):
    g = slice(f * LEV, (f + 1) * LEV)
    es[0, g], es[1, g] = fold_edges(x[BLOCKS - 1, g], x[0, g])


def edges_in(er, xh, xl):
    for side, block, turn in ((0, 0, 8), (1, BLOCKS + 1, 120)):
        v = er[side]
        for cols, part in ((slice(0, 128), v), (slice(128, 256), pltpu.roll(v, turn, 1))):
            hi, lo = split(part)
            xh[block, :, cols] = hi
            xl[block, :, cols] = lo


def pair_tables(owner, block, src, slot_of, slot_to, point_of, point_to, ids):
    pair, col = iota((PAIRS, 256), 0), iota((PAIRS, 256), 1) // 8

    def over_columns(column):
        return jnp.sum(jnp.where(pair == col, column, 0.0), axis=0, keepdims=True)

    eye = iota((PAIRS, PAIRS), 0) == iota((PAIRS, PAIRS), 1)

    def as_column(row):
        wide = jnp.broadcast_to(row.astype(f32), (PAIRS, PAIRS))
        return jnp.sum(jnp.where(eye, wide, 0.0), axis=1, keepdims=True)

    own = jnp.broadcast_to(as_column(owner[...]), (PAIRS, 256))
    own_c = over_columns(own)
    rank_c = jnp.sum(jnp.where((own == own_c) & (pair < col), 1.0, 0.0), axis=0, keepdims=True)
    slot_c = 2.0 * own_c + rank_c
    block_c = over_columns(jnp.broadcast_to(as_column(block[...]), (PAIRS, 256)))
    src_c = over_columns(jnp.broadcast_to(as_column(src[...]), (PAIRS, 256)))
    r, c = iota((256, 256), 0), iota((256, 256), 1)
    hit = ((r // 4).astype(f32) == slot_c) & ((r & 3) == (c & 7))
    table = hit.astype(f32)
    slot_of[...] = table.astype(bf16)
    slot_to[...] = table.T.astype(bf16)
    number = jnp.sum(table * (block_c + 1.0), axis=1, keepdims=True) - 1.0
    ids[...] = jnp.broadcast_to(number.astype(i32), (256, BLK)).reshape(DOM, 8, BLK)
    r, c = iota((64, 256), 0), iota((64, 256), 1)
    hit = ((r & 15).astype(f32) == src_c) & ((r // 16) == (c & 7))
    table = hit.astype(f32)
    point_of[...] = table.astype(bf16)
    point_to[...] = table.T.astype(bf16)


def pair_products(rows, wc, out, transposed):
    def body(i, _):
        for k in range(16):
            j = i * 16 + k
            v = rows[pl.ds(j * 8, 8), :]
            hi = v.astype(bf16).astype(f32)
            both = jnp.concatenate([hi, v - hi], axis=0).astype(bf16)
            if transposed:
                more = jnp.concatenate([hi, jnp.zeros_like(hi)], axis=0).astype(bf16)
                lhs = jnp.concatenate([both, more], axis=1)
                r = lax.dot_general(
                    lhs, wc[j], (((1,), (1,)), ((), ())), preferred_element_type=f32
                )
                out[pl.ds(j * 8, 8), :] = r[:8] + r[8:]
            else:
                r = jnp.dot(both, wc[j], preferred_element_type=f32)
                out[pl.ds(j * 8, 8), :] = r[:8, :BLK] + r[8:, :BLK] + r[:8, BLK:]
        return 0

    lax.fori_loop(0, PAIRS // 16, body, 0)


def kernel(
    state_hbm, weight_hbm, ocean_hbm,
    nbr_h, metric_h, coef_h, stiff_h, coup_h, vert_h, owner_h, block_h, src_h,
    cell_nbr_h, cell_diff_h, overt_h, mask_h,
    packed_hbm, ocean_out_hbm,
    nbr, metric, coef, stiff, coup, vert, owner, block, src,
    cell_nbr, cell_diff, overt, mask,
    st, x, xh, xl, y, yh, yl, vv, th, tl, met, cr, turned, near, delta, flux,
    wt, wc, rows_a, rows_b, slot_of, slot_to, point_of, point_to,
    es, er, es2, er2,
    ids_s, ids_r, rep_s, rep_r, flx_s, flx_r, surf_s, surf_r, ofl_s, ofl_r,
    oe, ob,
    small_sem, st_sem, wt_sem, oc_sem, out_sem,
    ids_ss, ids_rs, rep_ss, rep_rs, flx_ss, flx_rs,
    surf_ss, surf_rs, ofl_ss, ofl_rs,
    edge_ss, edge_rs, edge2_ss, edge2_rs, oh_ss, oh_rs,
):
    c, d = lax.axis_index("comp"), lax.axis_index("dom")
    barrier = pltpu.get_barrier_semaphore()
    ocean_slab = SLABS - 1

    def remote(src_ref, dst_ref, send, recv, comp, dom):
        return pltpu.make_async_remote_copy(
            src_ref=src_ref, dst_ref=dst_ref, send_sem=send, recv_sem=recv,
            device_id=(comp, dom), device_id_type=MESH,
        )

    def greet(comp, dom):
        pl.semaphore_signal(barrier, inc=1, device_id=(comp, dom), device_id_type=MESH)

    def fetch(pairs, first):
        copies = [
            pltpu.make_async_copy(a, b, small_sem.at[first + i]) for i, (a, b) in enumerate(pairs)
        ]
        for copy in copies:
            copy.start()
        return copies

    @pl.when(c < ATM)
    def _atmosphere():
        has_prev, has_next = (c + d) > 0, (c * DOM + d) < ATM * DOM - 1
        prev_c, prev_d = jnp.where(d == 0, c - 1, c), lax.rem(d + DOM - 1, DOM)
        next_c, next_d = jnp.where(d == DOM - 1, c + 1, c), lax.rem(d + 1, DOM)
        cross_prev = (d == 0) & (c > 0)
        cross_next = (d == DOM - 1) & (c < ATM - 1)

        def other(i):
            return lax.rem(d + i, DOM)

        def hello(i, _):
            greet(c, other(i))
            return 0

        state_in = [
            pltpu.make_async_copy(
                state_hbm.at[pl.ds(f * 2048, 2048)], st.at[pl.ds(f * 2048, 2048)], st_sem.at[f]
            )
            for f in range(FIELDS)
        ]
        state_in[0].start()
        lax.fori_loop(1, DOM, hello, 0, unroll=True)
        greet(ocean_slab, d)

        @pl.when(cross_prev)
        def _():
            greet(prev_c, prev_d)

        @pl.when(cross_next)
        def _():
            greet(next_c, next_d)

        for copy in state_in[1:]:
            copy.start()
        small_in = fetch(
            [(owner_h, owner), (block_h, block), (src_h, src), (nbr_h, nbr), (metric_h, metric),
             (coef_h, coef), (stiff_h, stiff), (coup_h, coup), (vert_h, vert)], 0,
        )
        weights_in = pltpu.make_async_copy(weight_hbm, wt, wt_sem)
        weights_in.start()

        def exchange(out, into, send, recv):
            def start():
                def body(i, _):
                    o = other(i)
                    remote(out.at[o], into.at[d], send, recv, c, o).start()
                    return 0

                into[d] = out[d]
                lax.fori_loop(1, DOM, body, 0, unroll=True)

            most = pl.ds(0, DOM - 1)
            every = remote(out.at[most], into.at[most], send, recv, c, other(1))
            return start, every.wait_recv, every.wait_send

        ids_start, ids_arrive, ids_sent = exchange(ids_s, ids_r, ids_ss, ids_rs)
        rep_start, rep_arrive, rep_sent = exchange(rep_s, rep_r, rep_ss, rep_rs)
        flx_start, flx_arrive, flx_sent = exchange(flx_s, flx_r, flx_ss, flx_rs)

        def edge_copies(out, into, send, recv, rows):
            up = remote(out.at[0, rows], into.at[0, rows], send.at[0], recv.at[0], next_c, next_d)
            down = remote(out.at[1, rows], into.at[1, rows], send.at[1], recv.at[1], prev_c, prev_d)

            def start():
                @pl.when(has_next)
                def _():
                    up.start()

                @pl.when(has_prev)
                def _():
                    down.start()

            def arrive():
                @pl.when(has_prev)
                def _():
                    up.wait_recv()

                @pl.when(has_next)
                def _():
                    down.wait_recv()

            def sent():
                @pl.when(has_next)
                def _():
                    up.wait_send()

                @pl.when(has_prev)
                def _():
                    down.wait_send()

            return start, arrive, sent

        edges = [
            edge_copies(es, er, edge_ss.at[f], edge_rs.at[f], pl.ds(f * LEV, LEV))
            for f in range(FIELDS)
        ]
        edge2_start, edge2_arrive, edge2_sent = edge_copies(
            es2, er2, edge2_ss, edge2_rs, pl.ds(0, ROWS)
        )

        @pl.when(jnp.logical_not(has_prev))
        def _():
            er[0] = jnp.zeros((ROWS, 128), f32)
            er2[0] = jnp.zeros((ROWS, 128), f32)

        @pl.when(jnp.logical_not(has_next))
        def _():
            er[1] = jnp.zeros((ROWS, 128), f32)
            er2[1] = jnp.zeros((ROWS, 128), f32)

        for copy in small_in:
            copy.wait()
        pair_tables(owner, block, src, slot_of, slot_to, point_of, point_to, ids_s)
        pl.semaphore_wait(
            barrier, DOM + jnp.where(cross_prev, 1, 0) + jnp.where(cross_next, 1, 0)
        )
        ids_start()
        for f in range(FIELDS):
            state_in[f].wait()
            pack(f, st, x, xh, xl)
            edges_out(f, x, es)
            edges[f][0]()

        small_tables(c * (DOM * ELEMS) + d * ELEMS, nbr, metric, stiff, coup, vert, cr, met, near, vv)

        def table(b, _):
            operator_block(b, near, cr, turned, th, tl)
            return 0

        lax.fori_loop(0, BLOCKS, table, 0)

        remote(surf_s, surf_r, surf_ss.at[0], surf_rs, ocean_slab, d).wait_recv()
        ids_arrive()

        def answer(i, _):
            which = ids_r[i]
            acc = jnp.zeros((8, BLK), f32)
            for b in range(OBLOCKS):
                acc = acc + jnp.where(which == b, surf_r[:, b * BLK : (b + 1) * BLK], 0.0)
            rep_s[i] = acc
            return 0

        lax.fori_loop(0, DOM, answer, 0, unroll=4)
        rep_start()

        weights_in.wait()

        def halves(j, _):
            hi, lo = split(wt[j])
            wc[j, :, :BLK] = hi
            wc[j, :, BLK:] = lo
            return 0

        lax.fori_loop(0, PAIRS, halves, 0, unroll=2)

        for b in (1, 2, 3, 4):
            advance(b, x, xh, xl, y, yh, yl, vv, th, tl, met)

        rep_arrive()
        rows_a[...] = pick_rows(slot_to[...], rep_r[...].reshape(256, BLK))
        pair_products(rows_a, wc, rows_b, True)
        surface = pick_rows(point_of[...], rows_b[...])
        top = jnp.concatenate(
            [st[f * 2048 + 2032 : f * 2048 + 2048, :] for f in range(FIELDS)], axis=0
        )
        fl = jnp.concatenate([coef[...]] * FIELDS, axis=0) * (top - surface)
        rows_a[...] = pick_rows(point_to[...], fl)
        pair_products(rows_a, wc, rows_b, False)
        flx_s[...] = pick_rows(slot_of[...], rows_b[...]).reshape(DOM, 8, BLK)
        flx_start()

        flux[:64] = fl * -0.5
        flux[64:] = jnp.zeros((64, BLK), f32)
        for h in range(2):
            w = to_blocks([flux[pl.ds(h * 8 + q, 8, stride=NPTS), :] for q in range(8)])
            for b in range(BLOCKS):
                delta[b, :, h * 128 : (h + 1) * 128] = w[b]
        for b in (1, 2, 3, 4):
            add_surface(b, delta, y, yh, yl)
        for f in range(FIELDS):
            edges[f][1]()
        edges_in(er, xh, xl)
        for b in (0, 7):
            advance(b, x, xh, xl, y, yh, yl, vv, th, tl, met, delta)
        for f in range(FIELDS):
            edges_out(f, y, es2)
        edge2_start()
        for b in (5, 6):
            advance(b, x, xh, xl, y, yh, yl, vv, th, tl, met, delta)

        def block_out(b):
            return pltpu.make_async_copy(x.at[b], packed_hbm.at[b], out_sem.at[b])

        def second(blocks):
            for b in blocks:
                advance(b, y, yh, yl, x, None, None, vv, th, tl, met, delta)
            for b in blocks:
                block_out(b).start()

        second((1, 2))
        flx_arrive()

        def gather(j, accs):
            which, val = ids_r[j], flx_r[j]
            return tuple(acc + jnp.where(which == b, val, 0.0) for b, acc in enumerate(accs))

        zero = jnp.zeros((8, BLK), f32)
        accs = lax.fori_loop(0, DOM, gather, (zero,) * OBLOCKS, unroll=4)
        for b in range(OBLOCKS):
            ofl_s[:, b * BLK : (b + 1) * BLK] = accs[b]
        remote(ofl_s, ofl_r.at[c], ofl_ss, ofl_rs.at[c], ocean_slab, d).start()
        second((3, 4, 5, 6))
        edge2_arrive()
        edges_in(er2, yh, yl)
        second((0, 7))
        ids_sent()
        rep_sent()
        flx_sent()
        for f in range(FIELDS):
            edges[f][2]()
        edge2_sent()
        remote(ofl_s, ofl_r.at[c], ofl_ss, ofl_rs.at[c], ocean_slab, d).wait_send()
        for b in range(BLOCKS):
            block_out(b).wait()

    @pl.when(c == ocean_slab)
    def _ocean():
        mid = oe.at[:, pl.ds(BLK, CELLS)]
        ocean_in = pltpu.make_async_copy(ocean_hbm, mid, oc_sem)
        ocean_in.start()
        small_in = fetch(
            [(cell_nbr_h, cell_nbr), (cell_diff_h, cell_diff), (overt_h, overt), (mask_h, mask)], 0
        )
        for comp in range(ATM):
            greet(comp, d)
        has_prev, has_next = d > 0, d < DOM - 1

        @pl.when(has_prev)
        def _():
            greet(c, d - 1)

        @pl.when(has_next)
        def _():
            greet(c, d + 1)

        ocean_in.wait()
        for k in range(2):
            for f in range(FIELDS):
                surf_s[k * 4 + f : k * 4 + f + 1, :] = oe[f * OLEV : f * OLEV + 1, BLK : BLK + CELLS]
        pl.semaphore_wait(
            barrier, ATM + jnp.where(has_prev, 1, 0) + jnp.where(has_next, 1, 0)
        )
        surf_out = [
            remote(surf_s, surf_r, surf_ss.at[comp], surf_rs, comp, d) for comp in range(ATM)
        ]
        for copy in surf_out:
            copy.start()
        up = remote(
            oe.at[:, pl.ds(CELLS, BLK)], oe.at[:, pl.ds(0, BLK)],
            oh_ss.at[0], oh_rs.at[0], c, lax.rem(d + 1, DOM),
        )
        down = remote(
            oe.at[:, pl.ds(BLK, BLK)], oe.at[:, pl.ds(CELLS + BLK, BLK)],
            oh_ss.at[1], oh_rs.at[1], c, lax.rem(d + DOM - 1, DOM),
        )

        @pl.when(has_next)
        def _():
            up.start()

        @pl.when(has_prev)
        def _():
            down.start()

        @pl.when(has_prev)
        def _():
            up.wait_recv()

        @pl.when(jnp.logical_not(has_prev))
        def _():
            oe[:, :BLK] = jnp.zeros((OROWS, BLK), f32)

        @pl.when(has_next)
        def _():
            down.wait_recv()

        @pl.when(jnp.logical_not(has_next))
        def _():
            oe[:, CELLS + BLK :] = jnp.zeros((OROWS, BLK), f32)

        for copy in small_in:
            copy.wait()
        source = iota((3 * BLK, BLK), 0)
        centre = source == iota((3 * BLK, BLK), 1) + BLK

        def cells(b, _):
            at = pl.multiple_of(b * BLK, BLK)
            here = pl.ds(at, BLK)
            rel = [cell_nbr[k, :, here] - (d * CELLS + at - BLK) for k in range(NBR_O)]
            diff = [cell_diff[k, :, here] for k in range(NBR_O)]
            mat = jnp.where(centre, jnp.broadcast_to(-sum(diff), (3 * BLK, BLK)), 0.0)
            for k in range(NBR_O):
                mat = mat + jnp.where(source == rel[k], diff[k], 0.0)
            lap = jnp.dot(
                oe[:, pl.ds(at, 3 * BLK)], mat, precision=highest, preferred_element_type=f32
            )
            for f in range(FIELDS):
                g = slice(f * OLEV, (f + 1) * OLEV)
                o = oe[g, pl.ds(at + BLK, BLK)]
                mix = jnp.dot(overt[...], o, precision=highest, preferred_element_type=f32)
                ob[g, here] = o + lap[g] + mix
            return 0

        lax.fori_loop(0, OBLOCKS, cells, 0)
        for comp in range(ATM):
            remote(ofl_s, ofl_r.at[comp], ofl_ss, ofl_rs.at[comp], comp, d).wait_recv()
        total = ofl_r[0] + ofl_r[1] + ofl_r[2]
        total = 0.5 * (total[:4] + total[4:])
        sea = mask[...] == 1
        first_row = iota((OLEV, CELLS), 0) == 0
        for f in range(FIELDS):
            g = slice(f * OLEV, (f + 1) * OLEV)
            fresh = ob[g, :] + jnp.where(first_row, total[f : f + 1, :], 0.0)
            ob[g, :] = jnp.where(sea, fresh, oe[g, BLK : BLK + CELLS])
        ocean_done = pltpu.make_async_copy(ob, ocean_out_hbm, out_sem.at[0])
        ocean_done.start()
        for copy in surf_out:
            copy.wait_send()

        @pl.when(has_next)
        def _():
            up.wait_send()

        @pl.when(has_prev)
        def _():
            down.wait_send()

        ocean_done.wait()


def finish(packed_hbm, ocean_hbm, atm_hbm, ocean_out_hbm, x, st, blank, in_sem, out_sem, oc_sem):
    c = lax.axis_index("comp")
    parts, levels = 8, ROWS // 8
    rows = levels * NPTS
    outs = [
        pltpu.make_async_copy(
            st.at[pl.ds(i * rows, rows)], atm_hbm.at[pl.ds(i * rows, rows)], out_sem.at[i]
        )
        for i in range(parts)
    ]

    @pl.when(c < ATM)
    def _():
        ins = [
            pltpu.make_async_copy(
                packed_hbm.at[:, pl.ds(i * levels, levels)],
                x.at[:, pl.ds(i * levels, levels)],
                in_sem.at[i],
            )
            for i in range(parts)
        ]
        for copy in ins:
            copy.start()
        blank[...] = jnp.zeros((OROWS, CELLS), f32)
        zero_out = pltpu.make_async_copy(blank, ocean_out_hbm, oc_sem)
        for i in range(parts):
            ins[i].wait()
            unpack(i * levels, levels, x, st)
            outs[i].start()
            if i == 2:
                zero_out.start()
        zero_out.wait()
        for copy in outs:
            copy.wait()

    @pl.when(c == ATM)
    def _():
        ocean_in = pltpu.make_async_copy(ocean_hbm, blank, in_sem.at[0])
        ocean_in.start()
        for i in range(parts):
            st[i * rows : (i + 1) * rows] = jnp.zeros((rows, ELEMS), f32)
            outs[i].start()
        ocean_in.wait()
        ocean_out = pltpu.make_async_copy(blank, ocean_out_hbm, oc_sem)
        ocean_out.start()
        ocean_out.wait()
        for copy in outs:
            copy.wait()


def local(
    atm_state, elem_nbr, elem_metric, bulk_coef, stiffness, coupling, atm_vertical,
    ocean_state, cell_nbr, cell_diff, ocean_vertical, sea_mask,
    pair_owner, pair_block, pair_src, remap_weight,
):
    vmem, sem = pltpu.VMEM, pltpu.SemaphoreType.DMA
    anywhere = pl.BlockSpec(memory_space=pl.ANY)
    big, halves = (BLOCKS, ROWS, LANES), (BLOCKS + 2, ROWS, LANES)
    message = (DOM, 8, BLK)
    scratch = [
        vmem((4, ELEMS), i32), vmem((NPTS, ELEMS), f32), vmem((NPTS, ELEMS), f32),
        vmem((NPTS, NPTS), f32), vmem((4, NPTS, NPTS), f32), vmem((LEV, LEV), f32),
        vmem((1, PAIRS), i32), vmem((1, PAIRS), i32), vmem((1, PAIRS), i32),
        vmem((NBR_O, 1, CELLS), i32), vmem((NBR_O, 1, CELLS), f32), vmem((OLEV, OLEV), f32),
        vmem((1, CELLS), i32),
        vmem((FIELDS * 2048, ELEMS), f32),
        vmem(big, f32), vmem(halves, bf16), vmem(halves, bf16),
        vmem(big, f32), vmem(halves, bf16), vmem(halves, bf16),
        vmem((2 * LEV, 2 * LEV), bf16), vmem((BLOCKS, 2 * LANES, LANES), bf16),
        vmem((BLOCKS, 2 * LANES, LANES), bf16), vmem((BLOCKS, 8, LANES), f32),
        vmem((5, NPTS, LANES), f32), vmem((5, NPTS, LANES), f32), vmem((BLOCKS, 8, 128), i32),
        vmem((BLOCKS, 8, LANES), f32), vmem((128, BLK), f32),
        vmem((PAIRS, BLK, BLK), f32), vmem((PAIRS, BLK, 2 * BLK), bf16),
        vmem((256, BLK), f32), vmem((256, BLK), f32),
        vmem((256, 256), bf16), vmem((256, 256), bf16), vmem((64, 256), bf16), vmem((256, 64), bf16),
        vmem((2, ROWS, 128), f32), vmem((2, ROWS, 128), f32),
        vmem((2, ROWS, 128), f32), vmem((2, ROWS, 128), f32),
        vmem(message, i32), vmem(message, i32), vmem(message, f32), vmem(message, f32),
        vmem(message, f32), vmem(message, f32),
        vmem((8, CELLS), f32), vmem((8, CELLS), f32), vmem((8, CELLS), f32),
        vmem((ATM, 8, CELLS), f32),
        vmem((OROWS, CELLS + 2 * BLK), f32), vmem((OROWS, CELLS), f32),
        sem((9,)), sem((FIELDS,)), sem, sem, sem((BLOCKS,)),
        sem, sem, sem, sem, sem, sem,
        sem((ATM,)), sem, sem, sem((ATM,)),
        sem((FIELDS, 2)), sem((FIELDS, 2)), sem((2,)), sem((2,)), sem((2,)), sem((2,)),
    ]
    packed, ocean = pl.pallas_call(
        kernel,
        out_shape=(jax.ShapeDtypeStruct(big, f32), jax.ShapeDtypeStruct((OROWS, CELLS), f32)),
        in_specs=[anywhere] * 16,
        out_specs=(anywhere, anywhere),
        scratch_shapes=scratch,
        compiler_params=pltpu.CompilerParams(
            collective_id=0, has_side_effects=True, vmem_limit_bytes=60 << 20
        ),
        name="coupled_step",
    )(
        atm_state.reshape(FIELDS * 2048, ELEMS),
        remap_weight[0],
        ocean_state.reshape(OROWS, CELLS),
        elem_nbr[0], elem_metric[0], bulk_coef[0], stiffness, coupling, atm_vertical,
        pair_owner.reshape(1, PAIRS), pair_block, pair_src,
        jnp.transpose(cell_nbr, (1, 0, 2)), jnp.transpose(cell_diff, (1, 0, 2)),
        ocean_vertical, sea_mask,
    )
    atm, ocean = pl.pallas_call(
        finish,
        out_shape=(
            jax.ShapeDtypeStruct((FIELDS * 2048, ELEMS), f32),
            jax.ShapeDtypeStruct((OROWS, CELLS), f32),
        ),
        in_specs=[anywhere] * 2,
        out_specs=(anywhere, anywhere),
        scratch_shapes=[
            vmem(big, f32), vmem((FIELDS * 2048, ELEMS), f32), vmem((OROWS, CELLS), f32),
            sem((8,)), sem((8,)), sem,
        ],
        compiler_params=pltpu.CompilerParams(vmem_limit_bytes=60 << 20),
        name="finish",
    )(packed, ocean)
    return (
        atm.reshape(1, FIELDS, LEV, NPTS, ELEMS),
        ocean.reshape(1, FIELDS, OLEV, CELLS),
    )


def solution(mesh):
    in_specs = (
        P("comp", None, None, None, "dom"),
        P("comp", None, "dom"),
        P("comp", None, "dom"),
        P("comp", None, "dom"),
        P(),
        P(),
        P(),
        P("comp", None, None, "dom"),
        P("comp", None, "dom"),
        P("comp", None, "dom"),
        P(),
        P("comp", "dom"),
        P("comp", "dom", None),
        P("comp", "dom"),
        P("comp", "dom"),
        P("comp", "dom", None, None),
    )
    out_specs = (P("comp", None, None, None, "dom"), P("comp", None, None, "dom"))
    return jax.shard_map(local, mesh=mesh, in_specs=in_specs, out_specs=out_specs, check_vma=False)
```

```python
import functools

import jax
import jax.numpy as jnp
from jax import lax
from jax.experimental import pallas as pl
from jax.experimental.pallas import tpu as pltpu
from jax.sharding import PartitionSpec as P

f32, bf16, i32 = jnp.float32, jnp.bfloat16, jnp.int32
FIELDS, LEV, NPTS, ELEMS = 4, 128, 16, 128
ROWS = FIELDS * LEV
BLOCKS, WIDTH = 8, 16
LANES = NPTS * WIDTH
SLABS, DOM = 4, 32
ATM = SLABS - 1
PAIRS, BLK = 32, 128
OLEV, CELLS, NBR_O = 80, 1024, 6
OROWS = FIELDS * OLEV
OBLOCKS = CELLS // BLK
MESH = pl.DeviceIdType.MESH
highest = lax.Precision.HIGHEST


def iota(shape, axis):
    return lax.broadcasted_iota(i32, shape, axis)


def exchange_chunks(a):
    chunk = iota(a[0].shape, 1) // WIDTH
    for k in (1, 2, 4):
        take = (chunk & k) != 0
        a = [jnp.where(take, a[(i + k) % 8], a[i]) for i in range(8)]
    return [a[(-b) % 8] for b in range(8)]


def to_blocks(a):
    return exchange_chunks([a[q] if q == 0 else pltpu.roll(a[q], WIDTH * q, 1) for q in range(8)])


def from_blocks(a):
    a = exchange_chunks(a)
    return [a[q] if q == 0 else pltpu.roll(a[q], 128 - WIDTH * q, 1) for q in range(8)]


def split(x):
    hi = x.astype(bf16)
    return hi, (x - hi.astype(f32)).astype(bf16)


def pick_rows(onehot, x):
    hi, lo = split(x)
    return jnp.dot(onehot, hi, preferred_element_type=f32) + jnp.dot(
        onehot, lo, preferred_element_type=f32
    )


def pack(f, st, x, xh, xl):
    def body(i, _):
        row = f * LEV + i * 16
        for h in range(2):
            a = [st[pl.ds(row * NPTS + h * 8 + q, 16, stride=NPTS), :] for q in range(8)]
            w = to_blocks(a)
            cols = slice(h * 128, (h + 1) * 128)
            for b in range(BLOCKS):
                hi, lo = split(w[b])
                x[b, pl.ds(row, 16), cols] = w[b]
                xh[b + 1, pl.ds(row, 16), cols] = hi
                xl[b + 1, pl.ds(row, 16), cols] = lo
        return 0

    lax.fori_loop(0, LEV // 16, body, 0, unroll=4)


def unpack(first, levels, x, st):
    def body(i, _):
        row = first + i * 16
        for h in range(2):
            cols = slice(h * 128, (h + 1) * 128)
            w = from_blocks([x[b, pl.ds(row, 16), cols] for b in range(BLOCKS)])
            for q in range(8):
                st[pl.ds(row * NPTS + h * 8 + q, 16, stride=NPTS), :] = w[q]
        return 0

    lax.fori_loop(0, levels // 16, body, 0, unroll=4)


def small_tables(first, nbr, metric, stiff, coup, vert, cr, met, near, vv):
    spread = (iota((NPTS, LANES), 0) == iota((NPTS, LANES), 1) // WIDTH).astype(f32)
    for s in range(5):
        mat = coup[s] if s < 4 else stiff[...]
        cr[s] = lax.dot_general(
            mat, spread, (((0,), (0,)), ((), ())), precision=highest, preferred_element_type=f32
        )
    for h in range(2):
        w = to_blocks(
            [jnp.broadcast_to(metric[h * 8 + q : h * 8 + q + 1, :], (8, 128)) for q in range(8)]
        )
        for b in range(BLOCKS):
            met[b, :, h * 128 : (h + 1) * 128] = w[b]
    own = jnp.concatenate([nbr[...], nbr[...]], axis=0) - first
    w = to_blocks([own] * 8)
    for b in range(BLOCKS):
        near[b] = w[b] - b * WIDTH
    hi, lo = split(vert[...])
    vv[:LEV, :LEV] = hi
    vv[:LEV, LEV:] = hi
    vv[LEV:, :LEV] = lo
    vv[LEV:, LEV:] = jnp.zeros((LEV, LEV), bf16)


def operator_block(b, near, cr, turned, th, tl):
    sub, lane = iota((WIDTH, LANES), 0), iota((WIDTH, LANES), 1)
    for s in range(5):
        for h in range(2):
            cols = slice(h * 128, (h + 1) * 128)
            turned[s, :, cols] = pltpu.roll(cr[s, :, cols], b * WIDTH, 1)
    rows = near[b]
    inner, outer = [], []
    for s in range(4):
        r = rows[s : s + 1, :]
        r = jnp.concatenate([r, r], axis=1)
        hit = sub == jnp.broadcast_to(r & (WIDTH - 1), (WIDTH, LANES))
        inside = jnp.broadcast_to((r >= 0) & (r < WIDTH), (WIDTH, LANES))
        inner.append(hit & inside)
        outer.append(hit & jnp.logical_not(inside))
    diag = sub == (lane & (WIDTH - 1))
    half = (WIDTH // 2, LANES)

    def row(s, q, shape):
        return jnp.broadcast_to(turned[s, pl.ds(q, 1), :], shape)

    for k in range(NPTS):
        h, chunk = k - k % 8, k % 8
        q = h + ((chunk - b + 8) & 7)
        after = h + ((chunk - b + 7) & 7)
        before = h + ((chunk - b + 9) & 7)
        c = jnp.where(diag, row(4, q, (WIDTH, LANES)), 0.0)
        d = jnp.zeros((WIDTH, LANES), f32)
        for s in range(4):
            c = c + jnp.where(inner[s], row(s, q, (WIDTH, LANES)), 0.0)
            sides = jnp.concatenate([row(s, after, half), row(s, before, half)], axis=0)
            d = d + jnp.where(outer[s], sides, 0.0)
        for base, part in ((0, c), (LANES, d)):
            hi, lo = split(part)
            here = slice(base + k * WIDTH, base + (k + 1) * WIDTH)
            th[b, here, :] = hi
            tl[b, here, :] = lo


def advance(b, x, xh, xl, y, yh, yl, vv, th, tl, met, delta=None):
    last = iota((16, LANES), 0) == 15
    low = (iota((ROWS, LANES), 1) & (WIDTH - 1)) < WIDTH // 2
    sh = jnp.where(low, xh[b + 2], xh[b])
    sl = jnp.where(low, xl[b + 2], xl[b])
    ch, cl = xh[b + 1], xl[b + 1]
    lhs = jnp.concatenate([ch, sh, cl, sl, ch, sh], axis=1)
    rhs = jnp.concatenate([th[b], th[b], tl[b]], axis=0)
    acc = jnp.dot(lhs, rhs, preferred_element_type=f32)
    for f in range(FIELDS):
        g = slice(f * LEV, (f + 1) * LEV)
        parts = jnp.concatenate([xh[b + 1, g], xl[b + 1, g]], axis=0)
        v = jnp.dot(vv[...], parts, preferred_element_type=f32)
        new = x[b, g] + met[b, 0:1, :] * (acc[g] + v[:LEV] + v[LEV:])
        if delta is not None:
            extra = jnp.broadcast_to(delta[b, f : f + 1, :], (16, LANES))
            tail = new[LEV - 16 :] + jnp.where(last, extra, 0.0)
            new = jnp.concatenate([new[: LEV - 16], tail], axis=0)
        y[b, g] = new
        if yh is not None:
            hi, lo = split(new)
            yh[b + 1, g] = hi
            yl[b + 1, g] = lo


def add_surface(b, delta, y, yh, yl):
    last = iota((16, LANES), 0) == 15
    for f in range(FIELDS):
        g = slice((f + 1) * LEV - 16, (f + 1) * LEV)
        new = y[b, g] + jnp.where(last, jnp.broadcast_to(delta[b, f : f + 1, :], (16, LANES)), 0.0)
        y[b, g] = new
        hi, lo = split(new)
        yh[b + 1, g] = hi
        yl[b + 1, g] = lo


def fold_edges(top, bottom):
    low = (iota((top.shape[0], 128), 1) & (WIDTH - 1)) < WIDTH // 2
    up = jnp.where(low, pltpu.roll(top[:, 128:], 120, 1), top[:, :128])
    down = jnp.where(low, bottom[:, :128], pltpu.roll(bottom[:, 128:], 8, 1))
    return up, down


def edges_out(f, x, es):
    g = slice(f * LEV, (f + 1) * LEV)
    es[0, g], es[1, g] = fold_edges(x[BLOCKS - 1, g], x[0, g])


def edges_in(er, xh, xl):
    for side, block, turn in ((0, 0, 8), (1, BLOCKS + 1, 120)):
        v = er[side]
        for cols, part in ((slice(0, 128), v), (slice(128, 256), pltpu.roll(v, turn, 1))):
            hi, lo = split(part)
            xh[block, :, cols] = hi
            xl[block, :, cols] = lo


def pair_tables(owner, block, src, slot_of, slot_to, point_of, point_to, ids):
    pair, col = iota((PAIRS, 256), 0), iota((PAIRS, 256), 1) // 8

    def over_columns(column):
        return jnp.sum(jnp.where(pair == col, column, 0.0), axis=0, keepdims=True)

    eye = iota((PAIRS, PAIRS), 0) == iota((PAIRS, PAIRS), 1)

    def as_column(row):
        wide = jnp.broadcast_to(row.astype(f32), (PAIRS, PAIRS))
        return jnp.sum(jnp.where(eye, wide, 0.0), axis=1, keepdims=True)

    own = jnp.broadcast_to(as_column(owner[...]), (PAIRS, 256))
    own_c = over_columns(own)
    rank_c = jnp.sum(jnp.where((own == own_c) & (pair < col), 1.0, 0.0), axis=0, keepdims=True)
    slot_c = 2.0 * own_c + rank_c
    block_c = over_columns(jnp.broadcast_to(as_column(block[...]), (PAIRS, 256)))
    src_c = over_columns(jnp.broadcast_to(as_column(src[...]), (PAIRS, 256)))
    r, c = iota((256, 256), 0), iota((256, 256), 1)
    hit = ((r // 4).astype(f32) == slot_c) & ((r & 3) == (c & 7))
    table = hit.astype(f32)
    slot_of[...] = table.astype(bf16)
    slot_to[...] = table.T.astype(bf16)
    number = jnp.sum(table * (block_c + 1.0), axis=1, keepdims=True) - 1.0
    ids[...] = jnp.broadcast_to(number.astype(i32), (256, BLK)).reshape(DOM, 8, BLK)
    r, c = iota((64, 256), 0), iota((64, 256), 1)
    hit = ((r & 15).astype(f32) == src_c) & ((r // 16) == (c & 7))
    table = hit.astype(f32)
    point_of[...] = table.astype(bf16)
    point_to[...] = table.T.astype(bf16)


def pair_products(rows, wc, out, transposed):
    def body(i, _):
        for k in range(16):
            j = i * 16 + k
            v = rows[pl.ds(j * 8, 8), :]
            hi = v.astype(bf16).astype(f32)
            both = jnp.concatenate([hi, v - hi], axis=0).astype(bf16)
            if transposed:
                more = jnp.concatenate([hi, jnp.zeros_like(hi)], axis=0).astype(bf16)
                lhs = jnp.concatenate([both, more], axis=1)
                r = lax.dot_general(
                    lhs, wc[j], (((1,), (1,)), ((), ())), preferred_element_type=f32
                )
                out[pl.ds(j * 8, 8), :] = r[:8] + r[8:]
            else:
                r = jnp.dot(both, wc[j], preferred_element_type=f32)
                out[pl.ds(j * 8, 8), :] = r[:8, :BLK] + r[8:, :BLK] + r[:8, BLK:]
        return 0

    lax.fori_loop(0, PAIRS // 16, body, 0)


def kernel(
    state_hbm, weight_hbm, ocean_hbm,
    nbr_h, metric_h, coef_h, stiff_h, coup_h, vert_h, owner_h, block_h, src_h,
    cell_nbr_h, cell_diff_h, overt_h, mask_h,
    packed_hbm, ocean_out_hbm,
    nbr, metric, coef, stiff, coup, vert, owner, block, src,
    cell_nbr, cell_diff, overt, mask,
    st, x, xh, xl, y, yh, yl, vv, th, tl, met, cr, turned, near, delta, flux,
    wt, wc, rows_a, rows_b, slot_of, slot_to, point_of, point_to,
    es, er, es2, er2,
    ids_s, ids_r, rep_s, rep_r, flx_s, flx_r, surf_s, surf_r, ofl_s, ofl_r,
    oe, ob,
    small_sem, st_sem, wt_sem, oc_sem, out_sem,
    ids_ss, ids_rs, rep_ss, rep_rs, flx_ss, flx_rs,
    surf_ss, surf_rs, ofl_ss, ofl_rs,
    edge_ss, edge_rs, edge2_ss, edge2_rs, oh_ss, oh_rs,
):
    c, d = lax.axis_index("comp"), lax.axis_index("dom")
    barrier = pltpu.get_barrier_semaphore()
    ocean_slab = SLABS - 1

    def remote(src_ref, dst_ref, send, recv, comp, dom):
        return pltpu.make_async_remote_copy(
            src_ref=src_ref, dst_ref=dst_ref, send_sem=send, recv_sem=recv,
            device_id=(comp, dom), device_id_type=MESH,
        )

    def greet(comp, dom):
        pl.semaphore_signal(barrier, inc=1, device_id=(comp, dom), device_id_type=MESH)

    def fetch(pairs, first):
        copies = [
            pltpu.make_async_copy(a, b, small_sem.at[first + i]) for i, (a, b) in enumerate(pairs)
        ]
        for copy in copies:
            copy.start()
        return copies

    @pl.when(c < ATM)
    def _atmosphere():
        has_prev, has_next = (c + d) > 0, (c * DOM + d) < ATM * DOM - 1
        prev_c, prev_d = jnp.where(d == 0, c - 1, c), lax.rem(d + DOM - 1, DOM)
        next_c, next_d = jnp.where(d == DOM - 1, c + 1, c), lax.rem(d + 1, DOM)
        cross_prev = (d == 0) & (c > 0)
        cross_next = (d == DOM - 1) & (c < ATM - 1)

        def other(i):
            return lax.rem(d + i, DOM)

        def hello(i, _):
            greet(c, other(i))
            return 0

        state_in = [
            pltpu.make_async_copy(
                state_hbm.at[pl.ds(f * 2048, 2048)], st.at[pl.ds(f * 2048, 2048)], st_sem.at[f]
            )
            for f in range(FIELDS)
        ]
        state_in[0].start()
        lax.fori_loop(1, DOM, hello, 0, unroll=True)
        greet(ocean_slab, d)

        @pl.when(cross_prev)
        def _():
            greet(prev_c, prev_d)

        @pl.when(cross_next)
        def _():
            greet(next_c, next_d)

        for copy in state_in[1:]:
            copy.start()
        small_in = fetch(
            [(owner_h, owner), (block_h, block), (src_h, src), (nbr_h, nbr), (metric_h, metric),
             (coef_h, coef), (stiff_h, stiff), (coup_h, coup), (vert_h, vert)], 0,
        )
        weights_in = pltpu.make_async_copy(weight_hbm, wt, wt_sem)
        weights_in.start()

        def exchange(out, into, send, recv):
            def start():
                def body(i, _):
                    o = other(i)
                    remote(out.at[o], into.at[d], send, recv, c, o).start()
                    return 0

                into[d] = out[d]
                lax.fori_loop(1, DOM, body, 0, unroll=True)

            most = pl.ds(0, DOM - 1)
            every = remote(out.at[most], into.at[most], send, recv, c, other(1))
            return start, every.wait_recv, every.wait_send

        ids_start, ids_arrive, ids_sent = exchange(ids_s, ids_r, ids_ss, ids_rs)
        rep_start, rep_arrive, rep_sent = exchange(rep_s, rep_r, rep_ss, rep_rs)
        flx_start, flx_arrive, flx_sent = exchange(flx_s, flx_r, flx_ss, flx_rs)

        def edge_copies(out, into, send, recv, rows):
            up = remote(out.at[0, rows], into.at[0, rows], send.at[0], recv.at[0], next_c, next_d)
            down = remote(out.at[1, rows], into.at[1, rows], send.at[1], recv.at[1], prev_c, prev_d)

            def start():
                @pl.when(has_next)
                def _():
                    up.start()

                @pl.when(has_prev)
                def _():
                    down.start()

            def arrive():
                @pl.when(has_prev)
                def _():
                    up.wait_recv()

                @pl.when(has_next)
                def _():
                    down.wait_recv()

            def sent():
                @pl.when(has_next)
                def _():
                    up.wait_send()

                @pl.when(has_prev)
                def _():
                    down.wait_send()

            return start, arrive, sent

        edges = [
            edge_copies(es, er, edge_ss.at[f], edge_rs.at[f], pl.ds(f * LEV, LEV))
            for f in range(FIELDS)
        ]
        edge2_start, edge2_arrive, edge2_sent = edge_copies(
            es2, er2, edge2_ss, edge2_rs, pl.ds(0, ROWS)
        )

        @pl.when(jnp.logical_not(has_prev))
        def _():
            er[0] = jnp.zeros((ROWS, 128), f32)
            er2[0] = jnp.zeros((ROWS, 128), f32)

        @pl.when(jnp.logical_not(has_next))
        def _():
            er[1] = jnp.zeros((ROWS, 128), f32)
            er2[1] = jnp.zeros((ROWS, 128), f32)

        for copy in small_in:
            copy.wait()
        pair_tables(owner, block, src, slot_of, slot_to, point_of, point_to, ids_s)
        pl.semaphore_wait(
            barrier, DOM + jnp.where(cross_prev, 1, 0) + jnp.where(cross_next, 1, 0)
        )
        ids_start()
        for f in range(FIELDS):
            state_in[f].wait()
            pack(f, st, x, xh, xl)
            edges_out(f, x, es)

        remote(surf_s, surf_r, surf_ss.at[0], surf_rs, ocean_slab, d).wait_recv()
        ids_arrive()

        def answer(i, _):
            which = ids_r[i]
            acc = jnp.zeros((8, BLK), f32)
            for b in range(OBLOCKS):
                acc = acc + jnp.where(which == b, surf_r[:, b * BLK : (b + 1) * BLK], 0.0)
            rep_s[i] = acc
            return 0

        lax.fori_loop(0, DOM, answer, 0, unroll=4)
        rep_start()
        for f in range(FIELDS):
            edges[f][0]()

        small_tables(c * (DOM * ELEMS) + d * ELEMS, nbr, metric, stiff, coup, vert, cr, met, near, vv)

        def table(b, _):
            operator_block(b, near, cr, turned, th, tl)
            return 0

        lax.fori_loop(0, BLOCKS, table, 0)


        weights_in.wait()

        def halves(j, _):
            hi, lo = split(wt[j])
            wc[j, :, :BLK] = hi
            wc[j, :, BLK:] = lo
            return 0

        lax.fori_loop(0, PAIRS, halves, 0, unroll=2)

        for b in (1, 2, 3, 4):
            advance(b, x, xh, xl, y, yh, yl, vv, th, tl, met)

        rep_arrive()
        rows_a[...] = pick_rows(slot_to[...], rep_r[...].reshape(256, BLK))
        pair_products(rows_a, wc, rows_b, True)
        surface = pick_rows(point_of[...], rows_b[...])
        top = jnp.concatenate(
            [st[f * 2048 + 2032 : f * 2048 + 2048, :] for f in range(FIELDS)], axis=0
        )
        fl = jnp.concatenate([coef[...]] * FIELDS, axis=0) * (top - surface)
        rows_a[...] = pick_rows(point_to[...], fl)
        pair_products(rows_a, wc, rows_b, False)
        flx_s[...] = pick_rows(slot_of[...], rows_b[...]).reshape(DOM, 8, BLK)
        flx_start()

        flux[:64] = fl * -0.5
        flux[64:] = jnp.zeros((64, BLK), f32)
        for h in range(2):
            w = to_blocks([flux[pl.ds(h * 8 + q, 8, stride=NPTS), :] for q in range(8)])
            for b in range(BLOCKS):
                delta[b, :, h * 128 : (h + 1) * 128] = w[b]
        for b in (1, 2, 3, 4):
            add_surface(b, delta, y, yh, yl)
        for f in range(FIELDS):
            edges[f][1]()
        edges_in(er, xh, xl)
        for b in (0, 7):
            advance(b, x, xh, xl, y, yh, yl, vv, th, tl, met, delta)
        for f in range(FIELDS):
            edges_out(f, y, es2)
        edge2_start()
        for b in (5, 6):
            advance(b, x, xh, xl, y, yh, yl, vv, th, tl, met, delta)

        def block_out(b):
            return pltpu.make_async_copy(x.at[b], packed_hbm.at[b], out_sem.at[b])

        def second(blocks):
            for b in blocks:
                advance(b, y, yh, yl, x, None, None, vv, th, tl, met, delta)
            for b in blocks:
                block_out(b).start()

        second((1, 2))
        flx_arrive()

        def gather(j, accs):
            which, val = ids_r[j], flx_r[j]
            return tuple(acc + jnp.where(which == b, val, 0.0) for b, acc in enumerate(accs))

        zero = jnp.zeros((8, BLK), f32)
        accs = lax.fori_loop(0, DOM, gather, (zero,) * OBLOCKS, unroll=4)
        for b in range(OBLOCKS):
            ofl_s[:, b * BLK : (b + 1) * BLK] = accs[b]
        remote(ofl_s, ofl_r.at[c], ofl_ss, ofl_rs.at[c], ocean_slab, d).start()
        second((3, 4, 5, 6))
        edge2_arrive()
        edges_in(er2, yh, yl)
        second((0, 7))
        ids_sent()
        rep_sent()
        flx_sent()
        for f in range(FIELDS):
            edges[f][2]()
        edge2_sent()
        remote(ofl_s, ofl_r.at[c], ofl_ss, ofl_rs.at[c], ocean_slab, d).wait_send()
        for b in range(BLOCKS):
            block_out(b).wait()

    @pl.when(c == ocean_slab)
    def _ocean():
        mid = oe.at[:, pl.ds(BLK, CELLS)]
        ocean_in = pltpu.make_async_copy(ocean_hbm, mid, oc_sem)
        ocean_in.start()
        small_in = fetch(
            [(cell_nbr_h, cell_nbr), (cell_diff_h, cell_diff), (overt_h, overt), (mask_h, mask)], 0
        )
        for comp in range(ATM):
            greet(comp, d)
        has_prev, has_next = d > 0, d < DOM - 1

        @pl.when(has_prev)
        def _():
            greet(c, d - 1)

        @pl.when(has_next)
        def _():
            greet(c, d + 1)

        ocean_in.wait()
        for k in range(2):
            for f in range(FIELDS):
                surf_s[k * 4 + f : k * 4 + f + 1, :] = oe[f * OLEV : f * OLEV + 1, BLK : BLK + CELLS]
        pl.semaphore_wait(
            barrier, ATM + jnp.where(has_prev, 1, 0) + jnp.where(has_next, 1, 0)
        )
        surf_out = [
            remote(surf_s, surf_r, surf_ss.at[comp], surf_rs, comp, d) for comp in range(ATM)
        ]
        for copy in surf_out:
            copy.start()
        up = remote(
            oe.at[:, pl.ds(CELLS, BLK)], oe.at[:, pl.ds(0, BLK)],
            oh_ss.at[0], oh_rs.at[0], c, lax.rem(d + 1, DOM),
        )
        down = remote(
            oe.at[:, pl.ds(BLK, BLK)], oe.at[:, pl.ds(CELLS + BLK, BLK)],
            oh_ss.at[1], oh_rs.at[1], c, lax.rem(d + DOM - 1, DOM),
        )

        @pl.when(has_next)
        def _():
            up.start()

        @pl.when(has_prev)
        def _():
            down.start()

        @pl.when(has_prev)
        def _():
            up.wait_recv()

        @pl.when(jnp.logical_not(has_prev))
        def _():
            oe[:, :BLK] = jnp.zeros((OROWS, BLK), f32)

        @pl.when(has_next)
        def _():
            down.wait_recv()

        @pl.when(jnp.logical_not(has_next))
        def _():
            oe[:, CELLS + BLK :] = jnp.zeros((OROWS, BLK), f32)

        for copy in small_in:
            copy.wait()
        source = iota((3 * BLK, BLK), 0)
        centre = source == iota((3 * BLK, BLK), 1) + BLK

        def cells(b, _):
            at = pl.multiple_of(b * BLK, BLK)
            here = pl.ds(at, BLK)
            rel = [cell_nbr[k, :, here] - (d * CELLS + at - BLK) for k in range(NBR_O)]
            diff = [cell_diff[k, :, here] for k in range(NBR_O)]
            mat = jnp.where(centre, jnp.broadcast_to(-sum(diff), (3 * BLK, BLK)), 0.0)
            for k in range(NBR_O):
                mat = mat + jnp.where(source == rel[k], diff[k], 0.0)
            lap = jnp.dot(
                oe[:, pl.ds(at, 3 * BLK)], mat, precision=highest, preferred_element_type=f32
            )
            for f in range(FIELDS):
                g = slice(f * OLEV, (f + 1) * OLEV)
                o = oe[g, pl.ds(at + BLK, BLK)]
                mix = jnp.dot(overt[...], o, precision=highest, preferred_element_type=f32)
                ob[g, here] = o + lap[g] + mix
            return 0

        lax.fori_loop(0, OBLOCKS, cells, 0)
        sea = mask[...] == 1
        done = []
        for f in range(FIELDS):
            g = slice(f * OLEV, (f + 1) * OLEV)
            ob[g, :] = jnp.where(sea, ob[g, :], oe[g, BLK : BLK + CELLS])
            rest = pl.ds(f * OLEV + 8, OLEV - 8)
            done.append(pltpu.make_async_copy(ob.at[rest], ocean_out_hbm.at[rest], out_sem.at[f]))
            done[-1].start()
        for comp in range(ATM):
            remote(ofl_s, ofl_r.at[comp], ofl_ss, ofl_rs.at[comp], comp, d).wait_recv()
        total = ofl_r[0] + ofl_r[1] + ofl_r[2]
        total = 0.5 * (total[:4] + total[4:])
        wet_top = (iota((8, CELLS), 0) == 0) & sea
        for f in range(FIELDS):
            g = slice(f * OLEV, f * OLEV + 8)
            ob[g, :] = ob[g, :] + jnp.where(wet_top, total[f : f + 1, :], 0.0)
            first = pl.ds(f * OLEV, 8)
            done.append(
                pltpu.make_async_copy(
                    ob.at[first], ocean_out_hbm.at[first], out_sem.at[FIELDS + f]
                )
            )
            done[-1].start()
        for copy in surf_out:
            copy.wait_send()

        @pl.when(has_next)
        def _():
            up.wait_send()

        @pl.when(has_prev)
        def _():
            down.wait_send()

        for copy in done:
            copy.wait()


def finish(packed_hbm, ocean_hbm, atm_hbm, ocean_out_hbm, x, st, blank, in_sem, out_sem, oc_sem):
    c = lax.axis_index("comp")
    parts, levels = 8, ROWS // 8
    rows = levels * NPTS
    outs = [
        pltpu.make_async_copy(
            st.at[pl.ds(i * rows, rows)], atm_hbm.at[pl.ds(i * rows, rows)], out_sem.at[i]
        )
        for i in range(parts)
    ]

    @pl.when(c < ATM)
    def _():
        ins = [
            pltpu.make_async_copy(
                packed_hbm.at[:, pl.ds(i * levels, levels)],
                x.at[:, pl.ds(i * levels, levels)],
                in_sem.at[i],
            )
            for i in range(parts)
        ]
        for copy in ins:
            copy.start()
        blank[...] = jnp.zeros((OROWS, CELLS), f32)
        zero_out = pltpu.make_async_copy(blank, ocean_out_hbm, oc_sem)
        for i in range(parts):
            ins[i].wait()
            unpack(i * levels, levels, x, st)
            outs[i].start()
            if i == 2:
                zero_out.start()
        zero_out.wait()
        for copy in outs:
            copy.wait()

    @pl.when(c == ATM)
    def _():
        ocean_in = pltpu.make_async_copy(ocean_hbm, blank, in_sem.at[0])
        ocean_in.start()
        for i in range(parts):
            st[i * rows : (i + 1) * rows] = jnp.zeros((rows, ELEMS), f32)
            outs[i].start()
        ocean_in.wait()
        ocean_out = pltpu.make_async_copy(blank, ocean_out_hbm, oc_sem)
        ocean_out.start()
        ocean_out.wait()
        for copy in outs:
            copy.wait()


def local(
    atm_state, elem_nbr, elem_metric, bulk_coef, stiffness, coupling, atm_vertical,
    ocean_state, cell_nbr, cell_diff, ocean_vertical, sea_mask,
    pair_owner, pair_block, pair_src, remap_weight,
):
    vmem, sem = pltpu.VMEM, pltpu.SemaphoreType.DMA
    anywhere = pl.BlockSpec(memory_space=pl.ANY)
    big, halves = (BLOCKS, ROWS, LANES), (BLOCKS + 2, ROWS, LANES)
    message = (DOM, 8, BLK)
    scratch = [
        vmem((4, ELEMS), i32), vmem((NPTS, ELEMS), f32), vmem((NPTS, ELEMS), f32),
        vmem((NPTS, NPTS), f32), vmem((4, NPTS, NPTS), f32), vmem((LEV, LEV), f32),
        vmem((1, PAIRS), i32), vmem((1, PAIRS), i32), vmem((1, PAIRS), i32),
        vmem((NBR_O, 1, CELLS), i32), vmem((NBR_O, 1, CELLS), f32), vmem((OLEV, OLEV), f32),
        vmem((1, CELLS), i32),
        vmem((FIELDS * 2048, ELEMS), f32),
        vmem(big, f32), vmem(halves, bf16), vmem(halves, bf16),
        vmem(big, f32), vmem(halves, bf16), vmem(halves, bf16),
        vmem((2 * LEV, 2 * LEV), bf16), vmem((BLOCKS, 2 * LANES, LANES), bf16),
        vmem((BLOCKS, 2 * LANES, LANES), bf16), vmem((BLOCKS, 8, LANES), f32),
        vmem((5, NPTS, LANES), f32), vmem((5, NPTS, LANES), f32), vmem((BLOCKS, 8, 128), i32),
        vmem((BLOCKS, 8, LANES), f32), vmem((128, BLK), f32),
        vmem((PAIRS, BLK, BLK), f32), vmem((PAIRS, BLK, 2 * BLK), bf16),
        vmem((256, BLK), f32), vmem((256, BLK), f32),
        vmem((256, 256), bf16), vmem((256, 256), bf16), vmem((64, 256), bf16), vmem((256, 64), bf16),
        vmem((2, ROWS, 128), f32), vmem((2, ROWS, 128), f32),
        vmem((2, ROWS, 128), f32), vmem((2, ROWS, 128), f32),
        vmem(message, i32), vmem(message, i32), vmem(message, f32), vmem(message, f32),
        vmem(message, f32), vmem(message, f32),
        vmem((8, CELLS), f32), vmem((8, CELLS), f32), vmem((8, CELLS), f32),
        vmem((ATM, 8, CELLS), f32),
        vmem((OROWS, CELLS + 2 * BLK), f32), vmem((OROWS, CELLS), f32),
        sem((9,)), sem((FIELDS,)), sem, sem, sem((BLOCKS,)),
        sem, sem, sem, sem, sem, sem,
        sem((ATM,)), sem, sem, sem((ATM,)),
        sem((FIELDS, 2)), sem((FIELDS, 2)), sem((2,)), sem((2,)), sem((2,)), sem((2,)),
    ]
    packed, ocean = pl.pallas_call(
        kernel,
        out_shape=(jax.ShapeDtypeStruct(big, f32), jax.ShapeDtypeStruct((OROWS, CELLS), f32)),
        in_specs=[anywhere] * 16,
        out_specs=(anywhere, anywhere),
        scratch_shapes=scratch,
        compiler_params=pltpu.CompilerParams(
            collective_id=0, has_side_effects=True, vmem_limit_bytes=60 << 20
        ),
        name="coupled_step",
    )(
        atm_state.reshape(FIELDS * 2048, ELEMS),
        remap_weight[0],
        ocean_state.reshape(OROWS, CELLS),
        elem_nbr[0], elem_metric[0], bulk_coef[0], stiffness, coupling, atm_vertical,
        pair_owner.reshape(1, PAIRS), pair_block, pair_src,
        jnp.transpose(cell_nbr, (1, 0, 2)), jnp.transpose(cell_diff, (1, 0, 2)),
        ocean_vertical, sea_mask,
    )
    atm, ocean = pl.pallas_call(
        finish,
        out_shape=(
            jax.ShapeDtypeStruct((FIELDS * 2048, ELEMS), f32),
            jax.ShapeDtypeStruct((OROWS, CELLS), f32),
        ),
        in_specs=[anywhere] * 2,
        out_specs=(anywhere, anywhere),
        scratch_shapes=[
            vmem(big, f32), vmem((FIELDS * 2048, ELEMS), f32), vmem((OROWS, CELLS), f32),
            sem((8,)), sem((8,)), sem,
        ],
        compiler_params=pltpu.CompilerParams(vmem_limit_bytes=60 << 20),
        name="finish",
    )(packed, ocean)
    return (
        atm.reshape(1, FIELDS, LEV, NPTS, ELEMS),
        ocean.reshape(1, FIELDS, OLEV, CELLS),
    )


def solution(mesh):
    in_specs = (
        P("comp", None, None, None, "dom"),
        P("comp", None, "dom"),
        P("comp", None, "dom"),
        P("comp", None, "dom"),
        P(),
        P(),
        P(),
        P("comp", None, None, "dom"),
        P("comp", None, "dom"),
        P("comp", None, "dom"),
        P(),
        P("comp", "dom"),
        P("comp", "dom", None),
        P("comp", "dom"),
        P("comp", "dom"),
        P("comp", "dom", None, None),
    )
    out_specs = (P("comp", None, None, None, "dom"), P("comp", None, None, "dom"))
    return jax.shard_map(local, mesh=mesh, in_specs=in_specs, out_specs=out_specs, check_vma=False)
```

```python
import functools

import jax
import jax.numpy as jnp
from jax import lax
from jax.experimental import pallas as pl
from jax.experimental.pallas import tpu as pltpu
from jax.sharding import PartitionSpec as P

f32, bf16, i32 = jnp.float32, jnp.bfloat16, jnp.int32
FIELDS, LEV, NPTS, ELEMS = 4, 128, 16, 128
ROWS = FIELDS * LEV
BLOCKS, WIDTH = 8, 16
LANES = NPTS * WIDTH
SLABS, DOM = 4, 32
ATM = SLABS - 1
PAIRS, BLK = 32, 128
OLEV, CELLS, NBR_O = 80, 1024, 6
OROWS = FIELDS * OLEV
OBLOCKS = CELLS // BLK
MESH = pl.DeviceIdType.MESH
highest = lax.Precision.HIGHEST


def iota(shape, axis):
    return lax.broadcasted_iota(i32, shape, axis)


def exchange_chunks(a):
    chunk = iota(a[0].shape, 1) // WIDTH
    for k in (1, 2, 4):
        take = (chunk & k) != 0
        a = [jnp.where(take, a[(i + k) % 8], a[i]) for i in range(8)]
    return [a[(-b) % 8] for b in range(8)]


def to_blocks(a):
    return exchange_chunks([a[q] if q == 0 else pltpu.roll(a[q], WIDTH * q, 1) for q in range(8)])


def from_blocks(a):
    a = exchange_chunks(a)
    return [a[q] if q == 0 else pltpu.roll(a[q], 128 - WIDTH * q, 1) for q in range(8)]


def split(x):
    hi = x.astype(bf16)
    return hi, (x - hi.astype(f32)).astype(bf16)


def pick_rows(onehot, x):
    hi, lo = split(x)
    return jnp.dot(onehot, hi, preferred_element_type=f32) + jnp.dot(
        onehot, lo, preferred_element_type=f32
    )


def pack(f, st, x, xh, xl):
    def body(i, _):
        row = f * LEV + i * 16
        for h in range(2):
            a = [st[pl.ds(row * NPTS + h * 8 + q, 16, stride=NPTS), :] for q in range(8)]
            w = to_blocks(a)
            cols = slice(h * 128, (h + 1) * 128)
            for b in range(BLOCKS):
                hi, lo = split(w[b])
                x[b, pl.ds(row, 16), cols] = w[b]
                xh[b + 1, pl.ds(row, 16), cols] = hi
                xl[b + 1, pl.ds(row, 16), cols] = lo
        return 0

    lax.fori_loop(0, LEV // 16, body, 0, unroll=4)


def unpack(first, levels, x, st):
    def body(i, _):
        row = first + i * 16
        for h in range(2):
            cols = slice(h * 128, (h + 1) * 128)
            w = from_blocks([x[b, pl.ds(row, 16), cols] for b in range(BLOCKS)])
            for q in range(8):
                st[pl.ds(row * NPTS + h * 8 + q, 16, stride=NPTS), :] = w[q]
        return 0

    lax.fori_loop(0, levels // 16, body, 0, unroll=4)


def small_tables(first, nbr, metric, stiff, coup, vert, cr, met, near, vv):
    spread = (iota((NPTS, LANES), 0) == iota((NPTS, LANES), 1) // WIDTH).astype(f32)
    for s in range(5):
        mat = coup[s] if s < 4 else stiff[...]
        cr[s] = lax.dot_general(
            mat, spread, (((0,), (0,)), ((), ())), precision=highest, preferred_element_type=f32
        )
    for h in range(2):
        w = to_blocks(
            [jnp.broadcast_to(metric[h * 8 + q : h * 8 + q + 1, :], (8, 128)) for q in range(8)]
        )
        for b in range(BLOCKS):
            met[b, :, h * 128 : (h + 1) * 128] = w[b]
    own = jnp.concatenate([nbr[...], nbr[...]], axis=0) - first
    w = to_blocks([own] * 8)
    for b in range(BLOCKS):
        near[b] = w[b] - b * WIDTH
    hi, lo = split(vert[...])
    vv[:LEV, :LEV] = hi
    vv[:LEV, LEV:] = hi
    vv[LEV:, :LEV] = lo
    vv[LEV:, LEV:] = jnp.zeros((LEV, LEV), bf16)


def operator_block(b, near, cr, turned, th, tl):
    sub, lane = iota((WIDTH, LANES), 0), iota((WIDTH, LANES), 1)
    for s in range(5):
        for h in range(2):
            cols = slice(h * 128, (h + 1) * 128)
            turned[s, :, cols] = pltpu.roll(cr[s, :, cols], b * WIDTH, 1)
    rows = near[b]
    inner, outer = [], []
    for s in range(4):
        r = rows[s : s + 1, :]
        r = jnp.concatenate([r, r], axis=1)
        hit = sub == jnp.broadcast_to(r & (WIDTH - 1), (WIDTH, LANES))
        inside = jnp.broadcast_to((r >= 0) & (r < WIDTH), (WIDTH, LANES))
        inner.append(hit & inside)
        outer.append(hit & jnp.logical_not(inside))
    diag = sub == (lane & (WIDTH - 1))
    half = (WIDTH // 2, LANES)

    def row(s, q, shape):
        return jnp.broadcast_to(turned[s, pl.ds(q, 1), :], shape)

    for k in range(NPTS):
        h, chunk = k - k % 8, k % 8
        q = h + ((chunk - b + 8) & 7)
        after = h + ((chunk - b + 7) & 7)
        before = h + ((chunk - b + 9) & 7)
        c = jnp.where(diag, row(4, q, (WIDTH, LANES)), 0.0)
        d = jnp.zeros((WIDTH, LANES), f32)
        for s in range(4):
            c = c + jnp.where(inner[s], row(s, q, (WIDTH, LANES)), 0.0)
            sides = jnp.concatenate([row(s, after, half), row(s, before, half)], axis=0)
            d = d + jnp.where(outer[s], sides, 0.0)
        for base, part in ((0, c), (LANES, d)):
            hi, lo = split(part)
            here = slice(base + k * WIDTH, base + (k + 1) * WIDTH)
            th[b, here, :] = hi
            tl[b, here, :] = lo


def advance(b, x, xh, xl, y, yh, yl, vv, th, tl, met, delta=None):
    last = iota((16, LANES), 0) == 15
    low = (iota((ROWS, LANES), 1) & (WIDTH - 1)) < WIDTH // 2
    sh = jnp.where(low, xh[b + 2], xh[b])
    sl = jnp.where(low, xl[b + 2], xl[b])
    ch, cl = xh[b + 1], xl[b + 1]
    lhs = jnp.concatenate([ch, sh, cl, sl, ch, sh], axis=1)
    rhs = jnp.concatenate([th[b], th[b], tl[b]], axis=0)
    acc = jnp.dot(lhs, rhs, preferred_element_type=f32)
    for f in range(FIELDS):
        g = slice(f * LEV, (f + 1) * LEV)
        parts = jnp.concatenate([xh[b + 1, g], xl[b + 1, g]], axis=0)
        v = jnp.dot(vv[...], parts, preferred_element_type=f32)
        new = x[b, g] + met[b, 0:1, :] * (acc[g] + v[:LEV] + v[LEV:])
        if delta is not None:
            extra = jnp.broadcast_to(delta[b, f : f + 1, :], (16, LANES))
            tail = new[LEV - 16 :] + jnp.where(last, extra, 0.0)
            new = jnp.concatenate([new[: LEV - 16], tail], axis=0)
        y[b, g] = new
        if yh is not None:
            hi, lo = split(new)
            yh[b + 1, g] = hi
            yl[b + 1, g] = lo


def add_surface(b, delta, y, yh, yl):
    last = iota((16, LANES), 0) == 15
    for f in range(FIELDS):
        g = slice((f + 1) * LEV - 16, (f + 1) * LEV)
        new = y[b, g] + jnp.where(last, jnp.broadcast_to(delta[b, f : f + 1, :], (16, LANES)), 0.0)
        y[b, g] = new
        hi, lo = split(new)
        yh[b + 1, g] = hi
        yl[b + 1, g] = lo


def fold_edges(top, bottom):
    low = (iota((top.shape[0], 128), 1) & (WIDTH - 1)) < WIDTH // 2
    up = jnp.where(low, pltpu.roll(top[:, 128:], 120, 1), top[:, :128])
    down = jnp.where(low, bottom[:, :128], pltpu.roll(bottom[:, 128:], 8, 1))
    return up, down


def edges_out(f, x, es):
    g = slice(f * LEV, (f + 1) * LEV)
    es[0, g], es[1, g] = fold_edges(x[BLOCKS - 1, g], x[0, g])


def edges_in(er, xh, xl):
    for side, block, turn in ((0, 0, 8), (1, BLOCKS + 1, 120)):
        v = er[side]
        for cols, part in ((slice(0, 128), v), (slice(128, 256), pltpu.roll(v, turn, 1))):
            hi, lo = split(part)
            xh[block, :, cols] = hi
            xl[block, :, cols] = lo


def pair_tables(owner, block, src, slot_of, slot_to, point_of, point_to, ids):
    pair, col = iota((PAIRS, 256), 0), iota((PAIRS, 256), 1) // 8

    def over_columns(column):
        return jnp.sum(jnp.where(pair == col, column, 0.0), axis=0, keepdims=True)

    eye = iota((PAIRS, PAIRS), 0) == iota((PAIRS, PAIRS), 1)

    def as_column(row):
        wide = jnp.broadcast_to(row.astype(f32), (PAIRS, PAIRS))
        return jnp.sum(jnp.where(eye, wide, 0.0), axis=1, keepdims=True)

    own = jnp.broadcast_to(as_column(owner[...]), (PAIRS, 256))
    own_c = over_columns(own)
    rank_c = jnp.sum(jnp.where((own == own_c) & (pair < col), 1.0, 0.0), axis=0, keepdims=True)
    slot_c = 2.0 * own_c + rank_c
    block_c = over_columns(jnp.broadcast_to(as_column(block[...]), (PAIRS, 256)))
    src_c = over_columns(jnp.broadcast_to(as_column(src[...]), (PAIRS, 256)))
    r, c = iota((256, 256), 0), iota((256, 256), 1)
    hit = ((r // 4).astype(f32) == slot_c) & ((r & 3) == (c & 7))
    table = hit.astype(f32)
    slot_of[...] = table.astype(bf16)
    slot_to[...] = table.T.astype(bf16)
    number = jnp.sum(table * (block_c + 1.0), axis=1, keepdims=True) - 1.0
    ids[...] = jnp.broadcast_to(number.astype(i32), (256, BLK)).reshape(DOM, 8, BLK)
    r, c = iota((64, 256), 0), iota((64, 256), 1)
    hit = ((r & 15).astype(f32) == src_c) & ((r // 16) == (c & 7))
    table = hit.astype(f32)
    point_of[...] = table.astype(bf16)
    point_to[...] = table.T.astype(bf16)


def pair_products(rows, wc, out, transposed):
    def body(i, _):
        for k in range(16):
            j = i * 16 + k
            v = rows[pl.ds(j * 8, 8), :]
            hi = v.astype(bf16).astype(f32)
            both = jnp.concatenate([hi, v - hi], axis=0).astype(bf16)
            if transposed:
                more = jnp.concatenate([hi, jnp.zeros_like(hi)], axis=0).astype(bf16)
                lhs = jnp.concatenate([both, more], axis=1)
                r = lax.dot_general(
                    lhs, wc[j], (((1,), (1,)), ((), ())), preferred_element_type=f32
                )
                out[pl.ds(j * 8, 8), :] = r[:8] + r[8:]
            else:
                r = jnp.dot(both, wc[j], preferred_element_type=f32)
                out[pl.ds(j * 8, 8), :] = r[:8, :BLK] + r[8:, :BLK] + r[:8, BLK:]
        return 0

    lax.fori_loop(0, PAIRS // 16, body, 0)


def kernel(
    state_hbm, weight_hbm, ocean_hbm,
    nbr_h, metric_h, coef_h, stiff_h, coup_h, vert_h, owner_h, block_h, src_h,
    cell_nbr_h, cell_diff_h, overt_h, mask_h,
    packed_hbm, ocean_out_hbm,
    nbr, metric, coef, stiff, coup, vert, owner, block, src,
    cell_nbr, cell_diff, overt, mask,
    st, x, xh, xl, y, yh, yl, vv, th, tl, met, cr, turned, near, delta, flux,
    wt, wc, rows_a, rows_b, slot_of, slot_to, point_of, point_to,
    es, er, es2, er2,
    ids_s, ids_r, rep_s, rep_r, flx_s, flx_r, surf_s, surf_r, ofl_s, ofl_r,
    oe, ob,
    small_sem, st_sem, wt_sem, oc_sem, out_sem,
    ids_ss, ids_rs, rep_ss, rep_rs, flx_ss, flx_rs,
    surf_ss, surf_rs, ofl_ss, ofl_rs,
    edge_ss, edge_rs, edge2_ss, edge2_rs, oh_ss, oh_rs,
):
    c, d = lax.axis_index("comp"), lax.axis_index("dom")
    barrier = pltpu.get_barrier_semaphore()
    ocean_slab = SLABS - 1

    def remote(src_ref, dst_ref, send, recv, comp, dom):
        return pltpu.make_async_remote_copy(
            src_ref=src_ref, dst_ref=dst_ref, send_sem=send, recv_sem=recv,
            device_id=(comp, dom), device_id_type=MESH,
        )

    def greet(comp, dom):
        pl.semaphore_signal(barrier, inc=1, device_id=(comp, dom), device_id_type=MESH)

    def fetch(pairs, first):
        copies = [
            pltpu.make_async_copy(a, b, small_sem.at[first + i]) for i, (a, b) in enumerate(pairs)
        ]
        for copy in copies:
            copy.start()
        return copies

    @pl.when(c < ATM)
    def _atmosphere():
        has_prev, has_next = (c + d) > 0, (c * DOM + d) < ATM * DOM - 1
        prev_c, prev_d = jnp.where(d == 0, c - 1, c), lax.rem(d + DOM - 1, DOM)
        next_c, next_d = jnp.where(d == DOM - 1, c + 1, c), lax.rem(d + 1, DOM)
        cross_prev = (d == 0) & (c > 0)
        cross_next = (d == DOM - 1) & (c < ATM - 1)

        def other(i):
            return lax.rem(d + i, DOM)

        def hello(i, _):
            greet(c, other(i))
            return 0

        state_in = [
            pltpu.make_async_copy(
                state_hbm.at[pl.ds(f * 2048, 2048)], st.at[pl.ds(f * 2048, 2048)], st_sem.at[f]
            )
            for f in range(FIELDS)
        ]
        state_in[0].start()
        lax.fori_loop(1, DOM, hello, 0, unroll=True)
        greet(ocean_slab, d)

        @pl.when(cross_prev)
        def _():
            greet(prev_c, prev_d)

        @pl.when(cross_next)
        def _():
            greet(next_c, next_d)

        for copy in state_in[1:]:
            copy.start()
        small_in = fetch(
            [(owner_h, owner), (block_h, block), (src_h, src), (nbr_h, nbr), (metric_h, metric),
             (coef_h, coef), (stiff_h, stiff), (coup_h, coup), (vert_h, vert)], 0,
        )
        weights_in = pltpu.make_async_copy(weight_hbm, wt, wt_sem)
        weights_in.start()

        def exchange(out, into, send, recv):
            def start():
                def body(i, _):
                    o = other(i)
                    remote(out.at[o], into.at[d], send, recv, c, o).start()
                    return 0

                into[d] = out[d]
                lax.fori_loop(1, DOM, body, 0, unroll=True)

            most = pl.ds(0, DOM - 1)
            every = remote(out.at[most], into.at[most], send, recv, c, other(1))
            return start, every.wait_recv, every.wait_send

        ids_start, ids_arrive, ids_sent = exchange(ids_s, ids_r, ids_ss, ids_rs)
        rep_start, rep_arrive, rep_sent = exchange(rep_s, rep_r, rep_ss, rep_rs)
        flx_start, flx_arrive, flx_sent = exchange(flx_s, flx_r, flx_ss, flx_rs)

        def edge_copies(out, into, send, recv, rows):
            up = remote(out.at[0, rows], into.at[0, rows], send.at[0], recv.at[0], next_c, next_d)
            down = remote(out.at[1, rows], into.at[1, rows], send.at[1], recv.at[1], prev_c, prev_d)

            def start():
                @pl.when(has_next)
                def _():
                    up.start()

                @pl.when(has_prev)
                def _():
                    down.start()

            def arrive():
                @pl.when(has_prev)
                def _():
                    up.wait_recv()

                @pl.when(has_next)
                def _():
                    down.wait_recv()

            def sent():
                @pl.when(has_next)
                def _():
                    up.wait_send()

                @pl.when(has_prev)
                def _():
                    down.wait_send()

            return start, arrive, sent

        edges = [
            edge_copies(es, er, edge_ss.at[f], edge_rs.at[f], pl.ds(f * LEV, LEV))
            for f in range(FIELDS)
        ]
        edge2_start, edge2_arrive, edge2_sent = edge_copies(
            es2, er2, edge2_ss, edge2_rs, pl.ds(0, ROWS)
        )

        @pl.when(jnp.logical_not(has_prev))
        def _():
            er[0] = jnp.zeros((ROWS, 128), f32)
            er2[0] = jnp.zeros((ROWS, 128), f32)

        @pl.when(jnp.logical_not(has_next))
        def _():
            er[1] = jnp.zeros((ROWS, 128), f32)
            er2[1] = jnp.zeros((ROWS, 128), f32)

        for copy in small_in:
            copy.wait()
        pair_tables(owner, block, src, slot_of, slot_to, point_of, point_to, ids_s)
        pl.semaphore_wait(
            barrier, DOM + jnp.where(cross_prev, 1, 0) + jnp.where(cross_next, 1, 0)
        )
        ids_start()
        for f in range(FIELDS):
            state_in[f].wait()
            pack(f, st, x, xh, xl)
            edges_out(f, x, es)

        remote(surf_s, surf_r, surf_ss.at[0], surf_rs, ocean_slab, d).wait_recv()
        ids_arrive()

        def answer(i, _):
            which = ids_r[i]
            acc = jnp.zeros((8, BLK), f32)
            for b in range(OBLOCKS):
                acc = acc + jnp.where(which == b, surf_r[:, b * BLK : (b + 1) * BLK], 0.0)
            rep_s[i] = acc
            return 0

        lax.fori_loop(0, DOM, answer, 0, unroll=4)
        rep_start()
        for f in range(FIELDS):
            edges[f][0]()

        small_tables(c * (DOM * ELEMS) + d * ELEMS, nbr, metric, stiff, coup, vert, cr, met, near, vv)

        def table(b, _):
            operator_block(b, near, cr, turned, th, tl)
            return 0

        lax.fori_loop(0, BLOCKS, table, 0)


        weights_in.wait()

        def halves(j, _):
            hi, lo = split(wt[j])
            wc[j, :, :BLK] = hi
            wc[j, :, BLK:] = lo
            return 0

        lax.fori_loop(0, PAIRS, halves, 0, unroll=2)

        for b in (1, 2, 3, 4):
            advance(b, x, xh, xl, y, yh, yl, vv, th, tl, met)

        rep_arrive()
        rows_a[...] = pick_rows(slot_to[...], rep_r[...].reshape(256, BLK))
        pair_products(rows_a, wc, rows_b, True)
        surface = pick_rows(point_of[...], rows_b[...])
        top = jnp.concatenate(
            [st[f * 2048 + 2032 : f * 2048 + 2048, :] for f in range(FIELDS)], axis=0
        )
        fl = jnp.concatenate([coef[...]] * FIELDS, axis=0) * (top - surface)
        rows_a[...] = pick_rows(point_to[...], fl)
        pair_products(rows_a, wc, rows_b, False)
        flx_s[...] = pick_rows(slot_of[...], rows_b[...]).reshape(DOM, 8, BLK)
        flx_start()

        flux[:64] = fl * -0.5
        flux[64:] = jnp.zeros((64, BLK), f32)
        for h in range(2):
            w = to_blocks([flux[pl.ds(h * 8 + q, 8, stride=NPTS), :] for q in range(8)])
            for b in range(BLOCKS):
                delta[b, :, h * 128 : (h + 1) * 128] = w[b]
        for f in range(FIELDS):
            edges[f][1]()
        edges_in(er, xh, xl)
        for b in (0, 7):
            advance(b, x, xh, xl, y, yh, yl, vv, th, tl, met, delta)
        for f in range(FIELDS):
            edges_out(f, y, es2)
        edge2_start()
        for b in (1, 2, 3, 4):
            add_surface(b, delta, y, yh, yl)
        for b in (5, 6):
            advance(b, x, xh, xl, y, yh, yl, vv, th, tl, met, delta)

        def block_out(b):
            return pltpu.make_async_copy(x.at[b], packed_hbm.at[b], out_sem.at[b])

        def second(blocks):
            for b in blocks:
                advance(b, y, yh, yl, x, None, None, vv, th, tl, met, delta)
            for b in blocks:
                block_out(b).start()

        second((1, 2))
        flx_arrive()

        def gather(j, accs):
            which, val = ids_r[j], flx_r[j]
            return tuple(acc + jnp.where(which == b, val, 0.0) for b, acc in enumerate(accs))

        zero = jnp.zeros((8, BLK), f32)
        accs = lax.fori_loop(0, DOM, gather, (zero,) * OBLOCKS, unroll=4)
        for b in range(OBLOCKS):
            ofl_s[:, b * BLK : (b + 1) * BLK] = accs[b]
        remote(ofl_s, ofl_r.at[c], ofl_ss, ofl_rs.at[c], ocean_slab, d).start()
        second((3, 4, 5, 6))
        edge2_arrive()
        edges_in(er2, yh, yl)
        second((0, 7))
        ids_sent()
        rep_sent()
        flx_sent()
        for f in range(FIELDS):
            edges[f][2]()
        edge2_sent()
        remote(ofl_s, ofl_r.at[c], ofl_ss, ofl_rs.at[c], ocean_slab, d).wait_send()
        for b in range(BLOCKS):
            block_out(b).wait()

    @pl.when(c == ocean_slab)
    def _ocean():
        mid = oe.at[:, pl.ds(BLK, CELLS)]
        ocean_in = pltpu.make_async_copy(ocean_hbm, mid, oc_sem)
        ocean_in.start()
        small_in = fetch(
            [(cell_nbr_h, cell_nbr), (cell_diff_h, cell_diff), (overt_h, overt), (mask_h, mask)], 0
        )
        for comp in range(ATM):
            greet(comp, d)
        has_prev, has_next = d > 0, d < DOM - 1

        @pl.when(has_prev)
        def _():
            greet(c, d - 1)

        @pl.when(has_next)
        def _():
            greet(c, d + 1)

        ocean_in.wait()
        for k in range(2):
            for f in range(FIELDS):
                surf_s[k * 4 + f : k * 4 + f + 1, :] = oe[f * OLEV : f * OLEV + 1, BLK : BLK + CELLS]
        pl.semaphore_wait(
            barrier, ATM + jnp.where(has_prev, 1, 0) + jnp.where(has_next, 1, 0)
        )
        surf_out = [
            remote(surf_s, surf_r, surf_ss.at[comp], surf_rs, comp, d) for comp in range(ATM)
        ]
        for copy in surf_out:
            copy.start()
        up = remote(
            oe.at[:, pl.ds(CELLS, BLK)], oe.at[:, pl.ds(0, BLK)],
            oh_ss.at[0], oh_rs.at[0], c, lax.rem(d + 1, DOM),
        )
        down = remote(
            oe.at[:, pl.ds(BLK, BLK)], oe.at[:, pl.ds(CELLS + BLK, BLK)],
            oh_ss.at[1], oh_rs.at[1], c, lax.rem(d + DOM - 1, DOM),
        )

        @pl.when(has_next)
        def _():
            up.start()

        @pl.when(has_prev)
        def _():
            down.start()

        @pl.when(has_prev)
        def _():
            up.wait_recv()

        @pl.when(jnp.logical_not(has_prev))
        def _():
            oe[:, :BLK] = jnp.zeros((OROWS, BLK), f32)

        @pl.when(has_next)
        def _():
            down.wait_recv()

        @pl.when(jnp.logical_not(has_next))
        def _():
            oe[:, CELLS + BLK :] = jnp.zeros((OROWS, BLK), f32)

        for copy in small_in:
            copy.wait()
        source = iota((3 * BLK, BLK), 0)
        centre = source == iota((3 * BLK, BLK), 1) + BLK

        def cells(b, _):
            at = pl.multiple_of(b * BLK, BLK)
            here = pl.ds(at, BLK)
            rel = [cell_nbr[k, :, here] - (d * CELLS + at - BLK) for k in range(NBR_O)]
            diff = [cell_diff[k, :, here] for k in range(NBR_O)]
            mat = jnp.where(centre, jnp.broadcast_to(-sum(diff), (3 * BLK, BLK)), 0.0)
            for k in range(NBR_O):
                mat = mat + jnp.where(source == rel[k], diff[k], 0.0)
            lap = jnp.dot(
                oe[:, pl.ds(at, 3 * BLK)], mat, precision=highest, preferred_element_type=f32
            )
            for f in range(FIELDS):
                g = slice(f * OLEV, (f + 1) * OLEV)
                o = oe[g, pl.ds(at + BLK, BLK)]
                mix = jnp.dot(overt[...], o, precision=highest, preferred_element_type=f32)
                ob[g, here] = o + lap[g] + mix
            return 0

        lax.fori_loop(0, OBLOCKS, cells, 0)
        sea = mask[...] == 1
        done = []
        for f in range(FIELDS):
            g = slice(f * OLEV, (f + 1) * OLEV)
            ob[g, :] = jnp.where(sea, ob[g, :], oe[g, BLK : BLK + CELLS])
            rest = pl.ds(f * OLEV + 8, OLEV - 8)
            done.append(pltpu.make_async_copy(ob.at[rest], ocean_out_hbm.at[rest], out_sem.at[f]))
            done[-1].start()
        for comp in range(ATM):
            remote(ofl_s, ofl_r.at[comp], ofl_ss, ofl_rs.at[comp], comp, d).wait_recv()
        total = ofl_r[0] + ofl_r[1] + ofl_r[2]
        total = 0.5 * (total[:4] + total[4:])
        wet_top = (iota((8, CELLS), 0) == 0) & sea
        for f in range(FIELDS):
            g = slice(f * OLEV, f * OLEV + 8)
            ob[g, :] = ob[g, :] + jnp.where(wet_top, total[f : f + 1, :], 0.0)
            first = pl.ds(f * OLEV, 8)
            done.append(
                pltpu.make_async_copy(
                    ob.at[first], ocean_out_hbm.at[first], out_sem.at[FIELDS + f]
                )
            )
            done[-1].start()
        for copy in surf_out:
            copy.wait_send()

        @pl.when(has_next)
        def _():
            up.wait_send()

        @pl.when(has_prev)
        def _():
            down.wait_send()

        for copy in done:
            copy.wait()


def finish(packed_hbm, ocean_hbm, atm_hbm, ocean_out_hbm, x, st, blank, in_sem, out_sem, oc_sem):
    c = lax.axis_index("comp")
    parts, levels = 8, ROWS // 8
    rows = levels * NPTS
    outs = [
        pltpu.make_async_copy(
            st.at[pl.ds(i * rows, rows)], atm_hbm.at[pl.ds(i * rows, rows)], out_sem.at[i]
        )
        for i in range(parts)
    ]

    @pl.when(c < ATM)
    def _():
        ins = [
            pltpu.make_async_copy(
                packed_hbm.at[:, pl.ds(i * levels, levels)],
                x.at[:, pl.ds(i * levels, levels)],
                in_sem.at[i],
            )
            for i in range(parts)
        ]
        for copy in ins:
            copy.start()
        blank[...] = jnp.zeros((OROWS, CELLS), f32)
        zero_out = pltpu.make_async_copy(blank, ocean_out_hbm, oc_sem)
        for i in range(parts):
            ins[i].wait()
            unpack(i * levels, levels, x, st)
            outs[i].start()
            if i == 2:
                zero_out.start()
        zero_out.wait()
        for copy in outs:
            copy.wait()

    @pl.when(c == ATM)
    def _():
        ocean_in = pltpu.make_async_copy(ocean_hbm, blank, in_sem.at[0])
        ocean_in.start()
        for i in range(parts):
            st[i * rows : (i + 1) * rows] = jnp.zeros((rows, ELEMS), f32)
            outs[i].start()
        ocean_in.wait()
        ocean_out = pltpu.make_async_copy(blank, ocean_out_hbm, oc_sem)
        ocean_out.start()
        ocean_out.wait()
        for copy in outs:
            copy.wait()


def local(
    atm_state, elem_nbr, elem_metric, bulk_coef, stiffness, coupling, atm_vertical,
    ocean_state, cell_nbr, cell_diff, ocean_vertical, sea_mask,
    pair_owner, pair_block, pair_src, remap_weight,
):
    vmem, sem = pltpu.VMEM, pltpu.SemaphoreType.DMA
    anywhere = pl.BlockSpec(memory_space=pl.ANY)
    big, halves = (BLOCKS, ROWS, LANES), (BLOCKS + 2, ROWS, LANES)
    message = (DOM, 8, BLK)
    scratch = [
        vmem((4, ELEMS), i32), vmem((NPTS, ELEMS), f32), vmem((NPTS, ELEMS), f32),
        vmem((NPTS, NPTS), f32), vmem((4, NPTS, NPTS), f32), vmem((LEV, LEV), f32),
        vmem((1, PAIRS), i32), vmem((1, PAIRS), i32), vmem((1, PAIRS), i32),
        vmem((NBR_O, 1, CELLS), i32), vmem((NBR_O, 1, CELLS), f32), vmem((OLEV, OLEV), f32),
        vmem((1, CELLS), i32),
        vmem((FIELDS * 2048, ELEMS), f32),
        vmem(big, f32), vmem(halves, bf16), vmem(halves, bf16),
        vmem(big, f32), vmem(halves, bf16), vmem(halves, bf16),
        vmem((2 * LEV, 2 * LEV), bf16), vmem((BLOCKS, 2 * LANES, LANES), bf16),
        vmem((BLOCKS, 2 * LANES, LANES), bf16), vmem((BLOCKS, 8, LANES), f32),
        vmem((5, NPTS, LANES), f32), vmem((5, NPTS, LANES), f32), vmem((BLOCKS, 8, 128), i32),
        vmem((BLOCKS, 8, LANES), f32), vmem((128, BLK), f32),
        vmem((PAIRS, BLK, BLK), f32), vmem((PAIRS, BLK, 2 * BLK), bf16),
        vmem((256, BLK), f32), vmem((256, BLK), f32),
        vmem((256, 256), bf16), vmem((256, 256), bf16), vmem((64, 256), bf16), vmem((256, 64), bf16),
        vmem((2, ROWS, 128), f32), vmem((2, ROWS, 128), f32),
        vmem((2, ROWS, 128), f32), vmem((2, ROWS, 128), f32),
        vmem(message, i32), vmem(message, i32), vmem(message, f32), vmem(message, f32),
        vmem(message, f32), vmem(message, f32),
        vmem((8, CELLS), f32), vmem((8, CELLS), f32), vmem((8, CELLS), f32),
        vmem((ATM, 8, CELLS), f32),
        vmem((OROWS, CELLS + 2 * BLK), f32), vmem((OROWS, CELLS), f32),
        sem((9,)), sem((FIELDS,)), sem, sem, sem((BLOCKS,)),
        sem, sem, sem, sem, sem, sem,
        sem((ATM,)), sem, sem, sem((ATM,)),
        sem((FIELDS, 2)), sem((FIELDS, 2)), sem((2,)), sem((2,)), sem((2,)), sem((2,)),
    ]
    packed, ocean = pl.pallas_call(
        kernel,
        out_shape=(jax.ShapeDtypeStruct(big, f32), jax.ShapeDtypeStruct((OROWS, CELLS), f32)),
        in_specs=[anywhere] * 16,
        out_specs=(anywhere, anywhere),
        scratch_shapes=scratch,
        compiler_params=pltpu.CompilerParams(
            collective_id=0, has_side_effects=True, vmem_limit_bytes=60 << 20
        ),
        name="coupled_step",
    )(
        atm_state.reshape(FIELDS * 2048, ELEMS),
        remap_weight[0],
        ocean_state.reshape(OROWS, CELLS),
        elem_nbr[0], elem_metric[0], bulk_coef[0], stiffness, coupling, atm_vertical,
        pair_owner.reshape(1, PAIRS), pair_block, pair_src,
        jnp.transpose(cell_nbr, (1, 0, 2)), jnp.transpose(cell_diff, (1, 0, 2)),
        ocean_vertical, sea_mask,
    )
    atm, ocean = pl.pallas_call(
        finish,
        out_shape=(
            jax.ShapeDtypeStruct((FIELDS * 2048, ELEMS), f32),
            jax.ShapeDtypeStruct((OROWS, CELLS), f32),
        ),
        in_specs=[anywhere] * 2,
        out_specs=(anywhere, anywhere),
        scratch_shapes=[
            vmem(big, f32), vmem((FIELDS * 2048, ELEMS), f32), vmem((OROWS, CELLS), f32),
            sem((8,)), sem((8,)), sem,
        ],
        compiler_params=pltpu.CompilerParams(vmem_limit_bytes=60 << 20),
        name="finish",
    )(packed, ocean)
    return (
        atm.reshape(1, FIELDS, LEV, NPTS, ELEMS),
        ocean.reshape(1, FIELDS, OLEV, CELLS),
    )


def solution(mesh):
    in_specs = (
        P("comp", None, None, None, "dom"),
        P("comp", None, "dom"),
        P("comp", None, "dom"),
        P("comp", None, "dom"),
        P(),
        P(),
        P(),
        P("comp", None, None, "dom"),
        P("comp", None, "dom"),
        P("comp", None, "dom"),
        P(),
        P("comp", "dom"),
        P("comp", "dom", None),
        P("comp", "dom"),
        P("comp", "dom"),
        P("comp", "dom", None, None),
    )
    out_specs = (P("comp", None, None, None, "dom"), P("comp", None, None, "dom"))
    return jax.shard_map(local, mesh=mesh, in_specs=in_specs, out_specs=out_specs, check_vma=False)
```
